512 devices in a mesh: dp: 32 (over z, x_hi, core), fsdp: 16 (over x_lo, y).
Axes of the slice: x: 4 (x_hi: 2, x_lo: 2; x = x_hi * 2 + x_lo), y: 8, z: 8, core: 2. Of those that a mesh axis runs over, the one named last changes fastest.
Arguments:
- activations: bfloat16 [98304, 4096], P(('dp', 'fsdp')), may hold values from -24 to 24
- cotangent: bfloat16 [98304, 512], P(('dp', 'fsdp')), may hold values from -6 to 6
- weight: bfloat16 [4096, 512], P('fsdp'), may hold values from -0.09375 to 0.09375
- momentum: float32 [32, 4096, 512], P('dp', 'fsdp'), may hold values from -256 to 256
- positions: int32 [16, 32, 512], P('fsdp'), may hold values from 0 to 255, as said below
Outputs:
- grad_input: bfloat16 [98304, 4096], P(('dp', 'fsdp'))
- new_momentum: float32 [32, 4096, 512], P('dp', 'fsdp')
- update: bfloat16 [4096, 512], P('fsdp')
The draws below stay inside these ranges and needn't reach their ends.
Inputs may be any that keep to these rules, and one draw needn't show every extreme that they name: For each block b and column c the 32 values positions[b, :, c] are distinct.
All inputs are finite; a program needn't handle non-finite values.
Results may differ from the reference program's by a relative error of at most 0.023.
Values may be sent and summed in bfloat16 or wider, within the bound.
A program may use at most 64 MiB of HBM per device.

```python
import jax
import jax.numpy as jnp
from jax import lax

D_WIN = 4096
KV = 512
SPAN = 256
TOPK = 32
TOK_DEV = 192
TOKENS = 98304
N_DP = 32
N_FSDP = 16


def draw_positions(key, part):
    shape = (D_WIN // SPAN, SPAN, KV)
    scores = jax.random.randint(key, shape, 0, 1 << 20, dtype=jnp.int32)
    ranked = scores * SPAN + lax.broadcasted_iota(jnp.int32, shape, 1)
    order = jnp.argsort(ranked, axis=1, stable=True)
    return order[:, :TOPK, :].astype(jnp.int32)


def strengthened(values, stream_key, source, target, shards_of, factor):
    def block_of(axis_at):
        return (jnp.arange(values.shape[axis_at]) // (values.shape[axis_at] // shards_of)).reshape((-1,) + (1,) * (values.ndim - 1 - axis_at))

    one_side = jax.random.permutation(stream_key, shards_of)[block_of(target)]
    second = (block_of(target) + shards_of // 2) % shards_of
    return jnp.where((block_of(source) == one_side) | (block_of(source) == second), factor * values, values)


def steps_of(rng, shape, shards, least, largest):
    level, own = 1.0, jax.random.fold_in(rng, 6)
    for axis_at, blocks in shards:
        draws = jnp.exp(jax.random.uniform(jax.random.fold_in(own, axis_at), (blocks,), jnp.float32, least / len(shards), largest / len(shards)))
        level = level * jnp.repeat(draws, shape[axis_at] // blocks).reshape([-1 if axis == axis_at else 1 for axis in range(len(shape))])
    return level


def centred(own_key, dims, deviation, reach, cuts=(), kind=jnp.bfloat16):
    factor_of = steps_of(own_key, dims, cuts, -0.22, 0.18) if cuts else 1.0
    array = jax.random.normal(own_key, dims, jnp.float32) * deviation * factor_of
    return jnp.minimum(jnp.maximum(array, -reach), reach).astype(kind)


def bell_draw_with(rng, shape, scale, bound, cuts, heavy, kind=jnp.bfloat16):
    result = scale * jax.random.normal(rng, shape, jnp.float32)
    if cuts:
        result = result * steps_of(rng, shape, cuts, -0.22, 0.18)
    return jnp.clip(strengthened(result, jax.random.fold_in(rng, 3), *heavy), -bound, bound).astype(kind)


def setup_inputs(seed: int = 0) -> dict:
    splits = jax.random.split(jax.random.key(seed), 6)
    return {
        "activations": bell_draw_with(splits[0], (TOKENS, D_WIN), 1.0, 24.0, ((0, 512),), (0, 1, 512, 6.0)),
        "cotangent": centred(splits[1], (TOKENS, KV), 1.0, 6.0, ((0, 512),)),
        "weight": centred(splits[2], (D_WIN, KV), D_WIN ** -0.5, 0.09375, ((0, 16),)),
        "momentum": centred(splits[3], (N_DP, D_WIN, KV), 40.0, 256.0, ((0, 32), (1, 16)), jnp.float32),
        "positions": draw_positions(jax.random.fold_in(splits[5], 71), 0),
    }


def transform_table(length):
    freq = jnp.arange(length, dtype=jnp.float32)[:, None]
    place = jnp.arange(length, dtype=jnp.float32)[None, :]
    angles = jnp.pi * (2.0 * place + 1.0) * freq / (2.0 * length)
    scales = jnp.where(freq == 0.0, jnp.sqrt(1.0 / length), jnp.sqrt(2.0 / length))
    return scales * jnp.cos(angles)

def forward_blocks(table, blocks):
    return jnp.einsum('kn,bnc->bkc', table, blocks, precision=lax.Precision.HIGHEST)

def inverse_blocks(table, coeffs):
    return jnp.einsum('kn,bkc->bnc', table, coeffs, precision=lax.Precision.HIGHEST)

def spread_band(values, positions, length):
    blocks, picks, columns = values.shape
    block_index = jnp.arange(blocks, dtype=jnp.int32)[:, None, None]
    column_index = jnp.arange(columns, dtype=jnp.int32)[None, None, :]
    dense = jnp.zeros((blocks, length, columns), values.dtype)
    return dense.at[block_index, positions, column_index].add(values)

def reference(activations, cotangent, weight, momentum, positions):
    table = transform_table(SPAN)
    inputs = activations.reshape(N_DP, N_FSDP, TOK_DEV, D_WIN)
    grads = cotangent.reshape(N_DP, N_FSDP, TOK_DEV, KV)

    def one_replica(packed):
        replica_inputs, replica_grads, replica_moment = packed
        flat_grads = replica_grads.reshape(N_FSDP * TOK_DEV, KV)
        grad_input = jnp.dot(flat_grads, weight.T, preferred_element_type=jnp.float32).astype(jnp.bfloat16)
        partials = jnp.einsum('stf,stj->sfj', replica_inputs.astype(jnp.float32), replica_grads.astype(jnp.float32))
        partials = partials.astype(jnp.bfloat16).astype(jnp.float32)
        gradient = lax.optimization_barrier(jnp.sum(partials, axis=0))
        moment = 0.999 * replica_moment + gradient
        blocks = moment.reshape(D_WIN // SPAN, SPAN, KV)
        coeffs = forward_blocks(table, blocks)
        picked = jnp.take_along_axis(coeffs, positions, axis=1)
        kept = blocks - inverse_blocks(table, spread_band(picked, positions, SPAN))
        return (grad_input, kept.reshape(D_WIN, KV), picked.astype(jnp.bfloat16))
    grad_input, new_momentum, bands = lax.map(one_replica, (inputs, grads, momentum))
    mean_band = lax.optimization_barrier(jnp.sum(bands.astype(jnp.float32), axis=0)) / N_DP
    update = inverse_blocks(table, spread_band(mean_band, positions, SPAN)).reshape(D_WIN, KV).astype(jnp.bfloat16)
    return (grad_input.reshape(N_DP * N_FSDP * TOK_DEV, D_WIN), new_momentum, update)
```

```python
import functools

import jax
import jax.numpy as jnp
import numpy as np
from jax import lax
from jax.experimental import pallas as pl
from jax.experimental.pallas import tpu as pltpu
from jax.sharding import PartitionSpec as P

NZ, NQ, NX, NY = 8, 4, 2, 8
SPAN, KV, TOPK, TOK, FEAT = 256, 512, 32, 192, 4096
HALF = FEAT // NX
SUBS = 4
MOMENTUM_DECAY = 0.999
MESH = pl.DeviceIdType.MESH
F32, BF16 = jnp.float32, jnp.bfloat16


def transform_table(length):
    freq = np.arange(length, dtype=np.float64)[:, None]
    place = np.arange(length, dtype=np.float64)[None, :]
    scales = np.where(freq == 0, np.sqrt(1.0 / length), np.sqrt(2.0 / length))
    return (scales * np.cos(np.pi * (2 * place + 1) * freq / (2 * length))).astype(np.float32)


def remote(src, dst, send, recv, dp, fsdp):
    return pltpu.make_async_remote_copy(
        src_ref=src, dst_ref=dst, send_sem=send, recv_sem=recv,
        device_id=(dp, fsdp), device_id_type=MESH,
    )


def meet(peers):
    barrier = pltpu.get_barrier_semaphore()
    for peer in peers:
        pl.semaphore_signal(barrier, inc=1, device_id=peer, device_id_type=MESH)
    pl.semaphore_wait(barrier, len(peers))


def exchange_kernel(
    a, c, w, pos, grad, full, inv,
    ax, cx, part, sbuf, rbuf, xs, xr, ys, yr, ws, wr, zs, zr, cs, cr, ls,
):
    d, f = lax.axis_index("dp"), lax.axis_index("fsdp")
    x, y = f // NY, lax.rem(f, NY)
    z, q = d // NQ, lax.rem(d, NQ)
    core = lax.rem(d, 2)
    piece = z * 2 + core
    other_x = lax.rem(f + NY, NX * NY)
    other_core = d + 1 - 2 * core

    def at_y(step):
        return x * NY + lax.rem(y + step + NY, NY)

    def at_z(step):
        return lax.rem(z + step + NZ, NZ) * NQ + q

    meet(
        [(d, other_x), (other_core, f), (at_z(1), f), (at_z(-1), f)]
        + [(d, at_y(o)) for o in range(1, NY)]
    )

    def cot_copy():
        return remote(c, cx, xs.at[8], xr.at[8], d, other_x)

    def act_copy(block):
        columns = pl.ds(pl.multiple_of((1 - x) * HALF + block * SPAN, SPAN), SPAN)
        return remote(a.at[:, columns], ax.at[block], xs.at[block], xr.at[block], d, other_x)

    def blocks_of(step):
        return lax.rem(y - 1 - step + 2 * NY, NY), lax.rem(y + 1 + step, NY)

    def own_piece(o):
        target = other_x if o == 0 else at_y(o)
        recv = wr.at[1, 0] if o == 0 else wr.at[0, o]
        return remote(w.at[piece], full.at[f, piece], ws.at[0, o], recv, d, target)

    def passed_piece(o):
        return remote(full.at[other_x, piece], full.at[other_x, piece], ws.at[1, o], wr.at[1, o], d, at_y(o))

    cot_copy().start()
    own_piece(0).start()
    for o in (4, 3, 5, 2, 6, 1, 7):
        own_piece(o).start()
    mine = pltpu.make_async_copy(w.at[piece], full.at[f, piece], ls)
    mine.start()
    for s in range(3):
        for block in blocks_of(s):
            act_copy(block).start()
    act_copy(lax.rem(y + 4, NY)).start()
    act_copy(y).start()

    @pl.loop(0, SPAN // 32)
    def _(r):
        rows = pl.ds(pl.multiple_of(r * 32, 32), 32)
        level = lax.broadcasted_iota(jnp.int32, (32, KV), 0) + r * 32
        total = jnp.full((32, KV), -1, jnp.int32)
        for i in range(TOPK):
            row = jnp.broadcast_to(pos[i : i + 1, :], (32, KV))
            total = jnp.where(row == level, i, total)
        inv[rows, :] = total

    def from_x():
        return remote(w.at[piece], full.at[other_x, piece], ws.at[0, 0], wr.at[1, 0], d, other_x)

    from_x().wait_recv()
    for o in (4, 3, 5, 2, 6, 1, 7):
        passed_piece(o).start()

    def piece_at(direction, step, which):
        at = lax.rem(z - step + NZ, NZ) if direction == 0 else lax.rem(z + step, NZ)
        return at * 2 + which

    def z_copy(direction, step, sub):
        shards = pl.ds(direction * 8 + sub * 4, 4)
        ref = full.at[shards, piece_at(direction, step, core)]
        return remote(
            ref, ref, zs.at[direction, step, sub], zr.at[direction, step, sub],
            at_z(1 if direction == 0 else -1), f,
        )

    def z_arrived(direction, step, sub):
        shards = pl.ds(direction * 8 + sub * 4, 4)
        ref = full.at[shards, piece_at(direction, step + 1, core)]
        return remote(
            ref, ref, zs.at[direction, step, sub], zr.at[direction, step, sub],
            at_z(1 if direction == 0 else -1), f,
        )

    def core_copy(direction, step):
        ref = full.at[pl.ds(direction * 8, 8), piece_at(direction, step, core)]
        return remote(ref, ref, cs.at[direction, step], cr.at[direction, step], other_core, f)

    def core_arrived(direction, step):
        ref = full.at[pl.ds(direction * 8, 8), piece_at(direction, step, 1 - core)]
        return remote(ref, ref, cs.at[direction, step], cr.at[direction, step], other_core, f)

    mine.wait()
    for o in range(1, NY):
        own = full.at[at_y(-o), piece]
        remote(own, own, ws.at[0, o], wr.at[0, o], d, at_y(o)).wait_recv()
        passed = full.at[lax.rem(at_y(-o) + NY, NX * NY), piece]
        remote(passed, passed, ws.at[1, o], wr.at[1, o], d, at_y(o)).wait_recv()
    for direction in range(2):
        for sub in range(2):
            z_copy(direction, 0, sub).start()
    for direction in range(2):
        core_copy(direction, 0).start()

    def product(block):
        act_copy(block).wait_recv()
        own = a[:, pl.ds(pl.multiple_of(x * HALF + block * SPAN, SPAN), SPAN)]
        dims = (((0,), (0,)), ((), ()))
        part[block] = lax.dot_general(own, c[...], dims, preferred_element_type=F32) + lax.dot_general(
            ax[block], cx[...], dims, preferred_element_type=F32
        )

    rows_of = SPAN // SUBS

    def y_copy(direction, step, sub):
        rows = pl.ds(sub * rows_of, rows_of)
        return remote(
            sbuf.at[direction, step, rows], rbuf.at[direction, step, rows],
            ys.at[direction, step, sub], yr.at[direction, step, sub],
            d, at_y(1 if direction == 0 else -1),
        )

    def y_send(step, first):
        blocks = blocks_of(step)
        for sub in range(SUBS):
            for direction in range(2):
                rows = pl.ds(sub * rows_of, rows_of)
                columns = pl.ds(direction * SPAN, SPAN)
                value = part[blocks[direction], rows, columns]
                if not first:
                    y_copy(direction, step - 1, sub).wait_recv()
                    value = value + rbuf[direction, step - 1, rows].astype(F32)
                sbuf[direction, step, rows] = value.astype(BF16)
                y_copy(direction, step, sub).start()

    cot_copy().wait_recv()
    for block in blocks_of(0):
        product(block)
    y_send(0, True)

    @pl.loop(1, 7)
    def _(step):
        back, ahead = blocks_of(step)

        @pl.when(step < 4)
        def _():
            product(back)

        @pl.when(step < 3)
        def _():
            product(ahead)

        @pl.when(step == 4)
        def _():
            product(y)

        y_send(step, False)
        for direction in range(2):
            for sub in range(2):
                z_arrived(direction, step - 1, sub).wait_recv()
                z_copy(direction, step, sub).start()
            core_copy(direction, step).start()

    for sub in range(SUBS):
        for direction in range(2):
            rows = pl.ds(sub * rows_of, rows_of)
            columns = pl.ds(direction * SPAN, SPAN)
            y_copy(direction, 6, sub).wait_recv()
            grad[rows, columns] = part[y, rows, columns] + rbuf[direction, 6, rows].astype(F32)
    for direction in range(2):
        for sub in range(2):
            z_arrived(direction, 6, sub).wait_recv()
        core_copy(direction, 7).start()

    cot_copy().wait_send()
    for o in range(NY):
        own_piece(o).wait_send()
    for o in range(1, NY):
        passed_piece(o).wait_send()

    @pl.loop(0, 8)
    def _(step):
        act_copy(step).wait_send()
        for direction in range(2):
            core_copy(direction, step).wait_send()
            core_arrived(direction, step).wait_recv()

    @pl.loop(0, 7)
    def _(step):
        for direction in range(2):
            for sub in range(SUBS):
                y_copy(direction, step, sub).wait_send()
            for sub in range(2):
                z_copy(direction, step, sub).wait_send()


def exchange(activations, cotangent, weight, positions):
    vmem = pl.BlockSpec(memory_space=pltpu.VMEM)
    dma = pltpu.SemaphoreType.DMA
    return pl.pallas_call(
        exchange_kernel,
        out_shape=(
            jax.ShapeDtypeStruct((SPAN, KV), F32),
            jax.ShapeDtypeStruct((16, 16, 16, KV), BF16),
            jax.ShapeDtypeStruct((SPAN, KV), jnp.int32),
        ),
        in_specs=[vmem] * 4,
        out_specs=(vmem, pl.BlockSpec(memory_space=pl.ANY), vmem),
        scratch_shapes=[
            pltpu.VMEM((NY, TOK, SPAN), BF16),
            pltpu.VMEM((TOK, KV), BF16),
            pltpu.VMEM((NY, SPAN, KV), F32),
            pltpu.VMEM((2, 7, SPAN, SPAN), BF16),
            pltpu.VMEM((2, 7, SPAN, SPAN), BF16),
            dma((9,)), dma((9,)),
            dma((2, 7, SUBS)), dma((2, 7, SUBS)),
            dma((2, NY)), dma((2, NY)),
            dma((2, 7, 2)), dma((2, 7, 2)),
            dma((2, 8)), dma((2, 8)),
            dma,
        ],
        compiler_params=pltpu.CompilerParams(
            collective_id=0, has_side_effects=True, vmem_limit_bytes=32 << 20
        ),
        name="exchange",
    )(activations, cotangent, weight.reshape(16, 16, KV), positions)


def pick_rows(values, where, groups):
    low, high = where & 7, where >> 3
    found = jnp.zeros(where.shape, values.dtype)
    for group in range(groups):
        rows = jnp.take_along_axis(values[group * 8 : group * 8 + 8, :], low, axis=0)
        found = jnp.where(high == group, rows, found)
    return found


def dot_full(left, right, dims):
    return lax.dot_general(
        left, right, (dims, ((), ())), precision=lax.Precision.HIGHEST, preferred_element_type=F32
    )


def momentum_kernel(table, grad, momentum, pos, inv, kept, bands, coeffs):
    moment = MOMENTUM_DECAY * momentum[0] + grad[...]
    found = dot_full(table[...], moment, ((1,), (0,)))
    coeffs[...] = found
    masked = jnp.where(inv[...] >= 0, found, 0.0)
    for column in range(KV // 128):
        lanes = pl.ds(column * 128, 128)
        picked = [
            pick_rows(coeffs[:, lanes], pos[pl.ds(r * 8, 8), lanes], SPAN // 8) for r in range(TOPK // 8)
        ]
        bands[:, lanes] = jnp.concatenate(picked, axis=0).astype(BF16)
    kept[0] = moment - dot_full(table[...], masked, ((0,), (0,)))


def step_momentum(table, grad, momentum, positions, inv):
    vmem = pl.BlockSpec(memory_space=pltpu.VMEM)
    return pl.pallas_call(
        momentum_kernel,
        out_shape=(
            jax.ShapeDtypeStruct((1, SPAN, KV), F32),
            jax.ShapeDtypeStruct((TOPK, KV), BF16),
        ),
        in_specs=[vmem] * 5,
        out_specs=(vmem, vmem),
        scratch_shapes=[pltpu.VMEM((SPAN, KV), F32)],
        name="momentum",
    )(table, grad, momentum, positions, inv)


def bands_kernel(bands, c, full, mean, out, first, second, total, third, ss, sr):
    d, f = lax.axis_index("dp"), lax.axis_index("fsdp")
    z, q = d // NQ, lax.rem(d, NQ)
    hi, core = q // 2, lax.rem(q, 2)

    def at_q(k):
        flip_hi, flip_core = k // 2, k % 2
        new_hi = 1 - hi if flip_hi else hi
        new_core = 1 - core if flip_core else core
        return new_hi * 2 + new_core

    def at_z(step):
        return lax.rem(z + step + NZ, NZ)

    meet([(z * NQ + at_q(k), f) for k in range(1, 4)] + [(at_z(o) * NQ + q, f) for o in range(1, NZ)])

    def one(k):
        columns = pl.ds(pl.multiple_of(at_q(k) * 128, 128), 128)
        return remote(bands.at[:, columns], first.at[k - 1], ss.at[0, k], sr.at[0, k], z * NQ + at_q(k), f)

    def two(o):
        return remote(total, second.at[z], ss.at[1, o], sr.at[1, o], at_z(o) * NQ + q, f)

    def two_arrived(o):
        return remote(total, second.at[at_z(-o)], ss.at[1, o], sr.at[1, o], at_z(o) * NQ + q, f)

    def three(k):
        return remote(third.at[q], third.at[q], ss.at[2, k], sr.at[2, k], z * NQ + at_q(k), f)

    def three_arrived(k):
        slot = third.at[at_q(k)]
        return remote(slot, slot, ss.at[2, k], sr.at[2, k], z * NQ + at_q(k), f)

    def products(low, high):
        @pl.loop(low, high)
        def _(tile):
            rows = pl.ds(pl.multiple_of(tile * 512, 512), 512)
            out[:, rows] = lax.dot_general(
                c[...], full[rows, :], (((1,), (1,)), ((), ())), preferred_element_type=F32
            ).astype(BF16)

    for k in (3, 2, 1):
        one(k).start()
    products(0, 2)
    summed = bands[:, pl.ds(pl.multiple_of(q * 128, 128), 128)].astype(F32)
    for k in (1, 2, 3):
        one(k).wait_recv()
        summed = summed + first[k - 1].astype(F32)
    total[...] = summed
    for o in (4, 3, 5, 2, 6, 1, 7):
        two(o).start()
    second[z] = summed
    products(2, 6)
    for o in range(1, NZ):
        two_arrived(o).wait_recv()
    summed = second[0]
    for at in range(1, NZ):
        summed = summed + second[at]
    third[q] = summed / 32.0
    for k in (3, 2, 1):
        three(k).start()
    products(6, 8)
    for k in (1, 2, 3):
        three_arrived(k).wait_recv()
    for at in range(NQ):
        mean[:, at * 128 : at * 128 + 128] = third[at]
    for k in (1, 2, 3):
        one(k).wait_send()
        three(k).wait_send()
    for o in range(1, NZ):
        two(o).wait_send()


def reduce_bands(bands, cotangent, full):
    vmem = pl.BlockSpec(memory_space=pltpu.VMEM)
    dma = pltpu.SemaphoreType.DMA
    return pl.pallas_call(
        bands_kernel,
        out_shape=(
            jax.ShapeDtypeStruct((TOPK, KV), F32),
            jax.ShapeDtypeStruct((TOK, FEAT), BF16),
        ),
        in_specs=[vmem] * 3,
        out_specs=(vmem, vmem),
        scratch_shapes=[
            pltpu.VMEM((3, TOPK, 128), BF16),
            pltpu.VMEM((NZ, TOPK, 128), F32),
            pltpu.VMEM((TOPK, 128), F32),
            pltpu.VMEM((NQ, TOPK, 128), F32),
            dma((3, 8)), dma((3, 8)),
        ],
        compiler_params=pltpu.CompilerParams(
            collective_id=1, has_side_effects=True, vmem_limit_bytes=32 << 20
        ),
        name="bands",
    )(bands, cotangent, full)


def update_kernel(table, mean, inv, given, update, result, dense, sem):
    copy = pltpu.make_async_copy(given, result, sem)
    copy.start()
    for column in range(KV // 128):
        lanes = pl.ds(column * 128, 128)
        for r in range(SPAN // 8):
            dense[pl.ds(r * 8, 8), lanes] = pick_rows(mean[:, lanes], inv[pl.ds(r * 8, 8), lanes], TOPK // 8)
    update[...] = dot_full(table[...], dense[...], ((0,), (0,))).astype(BF16)
    copy.wait()


def decode(table, mean, inv, given):
    vmem = pl.BlockSpec(memory_space=pltpu.VMEM)
    return pl.pallas_call(
        update_kernel,
        out_shape=(
            jax.ShapeDtypeStruct((SPAN, KV), BF16),
            jax.ShapeDtypeStruct((TOK, FEAT), BF16),
        ),
        in_specs=[vmem] * 4,
        out_specs=(vmem, pl.BlockSpec(memory_space=pl.ANY)),
        scratch_shapes=[pltpu.VMEM((SPAN, KV), F32), pltpu.SemaphoreType.DMA],
        name="decode",
    )(table, mean, inv, given)


def on_device(activations, cotangent, weight, momentum, positions):
    table = jnp.asarray(transform_table(SPAN))
    where = positions[0]
    grad, full, inv = exchange(activations, cotangent, weight, where)
    kept, bands = step_momentum(table, grad, momentum, where, inv)
    mean, product = reduce_bands(bands, cotangent, full.reshape(FEAT, KV))
    update, grad_input = decode(table, mean, inv, product)
    return grad_input, kept, update


def solution(mesh):
    placed = (
        P(("dp", "fsdp"), None),
        P(("dp", "fsdp"), None),
        P("fsdp", None),
        P("dp", "fsdp", None),
        P("fsdp", None, None),
    )
    return jax.shard_map(
        on_device,
        mesh=mesh,
        in_specs=placed,
        out_specs=(P(("dp", "fsdp"), None), P("dp", "fsdp", None), P("fsdp", None)),
        check_vma=False,
    )
```

```python
import functools

import jax
import jax.numpy as jnp
import numpy as np
from jax import lax
from jax.experimental import pallas as pl
from jax.experimental.pallas import tpu as pltpu
from jax.sharding import PartitionSpec as P

NZ, NQ, NX, NY = 8, 4, 2, 8
SPAN, KV, TOPK, TOK, FEAT = 256, 512, 32, 192, 4096
HALF = FEAT // NX
SUBS = 4
TOKENS_IN = (((0,), (0,)), ((), ()))
MOMENTUM_DECAY = 0.999
MESH = pl.DeviceIdType.MESH
F32, BF16 = jnp.float32, jnp.bfloat16


def transform_table(length):
    freq = np.arange(length, dtype=np.float64)[:, None]
    place = np.arange(length, dtype=np.float64)[None, :]
    scales = np.where(freq == 0, np.sqrt(1.0 / length), np.sqrt(2.0 / length))
    return (scales * np.cos(np.pi * (2 * place + 1) * freq / (2 * length))).astype(np.float32)


def remote(src, dst, send, recv, dp, fsdp):
    return pltpu.make_async_remote_copy(
        src_ref=src, dst_ref=dst, send_sem=send, recv_sem=recv,
        device_id=(dp, fsdp), device_id_type=MESH,
    )


def meet(peers):
    barrier = pltpu.get_barrier_semaphore()
    for peer in peers:
        pl.semaphore_signal(barrier, inc=1, device_id=peer, device_id_type=MESH)
    pl.semaphore_wait(barrier, len(peers))


def pick_rows(values, where, groups):
    low, high = where & 7, where >> 3
    found = jnp.zeros(where.shape, values.dtype)
    for group in range(groups):
        rows = jnp.take_along_axis(values[group * 8 : group * 8 + 8, :], low, axis=0)
        found = jnp.where(high == group, rows, found)
    return found


def dot_full(left, right, dims):
    return lax.dot_general(
        left, right, (dims, ((), ())), precision=lax.Precision.HIGHEST, preferred_element_type=F32
    )


def step_kernel(
    a, c, w, momentum, positions, table,
    kept, out, mean, inv,
    av, cv, pos, tv, mv, ax, cx, part, full, half_s, half_r, block_s, block_r,
    coeffs, bands, first, total, second, third,
    ls, xs, xr, hs, hr, ys, yr, ws, wr, zs, zr, cs, cr, ss, sr,
):
    d, f = lax.axis_index("dp"), lax.axis_index("fsdp")
    x, y = f // NY, lax.rem(f, NY)
    z, q = d // NQ, lax.rem(d, NQ)
    hi, core = q // 2, lax.rem(q, 2)
    piece = z * 2 + core
    other_x = lax.rem(f + NY, NX * NY)
    other_core = d + 1 - 2 * core

    def wrap_y(at):
        return lax.rem(at + 2 * NY, NY)

    def wrap_z(at):
        return lax.rem(at + 2 * NZ, NZ)

    def at_y(step):
        return x * NY + wrap_y(y + step)

    def at_z(step):
        return wrap_z(z + step) * NQ + q

    def at_q(k):
        new_hi = 1 - hi if k // 2 else hi
        new_core = 1 - core if k % 2 else core
        return new_hi * 2 + new_core

    local = [
        pltpu.make_async_copy(positions, pos, ls.at[0]),
        pltpu.make_async_copy(c, cv, ls.at[1]),
        pltpu.make_async_copy(a.at[:, pl.ds(pl.multiple_of(x * HALF, HALF), HALF)], av, ls.at[2]),
        pltpu.make_async_copy(w.at[piece], full.at[f, piece], ls.at[3]),
        pltpu.make_async_copy(table, tv, ls.at[4]),
        pltpu.make_async_copy(momentum, mv, ls.at[5]),
    ]
    for copy in local:
        copy.start()

    meet(
        [(d, other_x)]
        + [(d, at_y(o)) for o in range(1, NY)]
        + [(at_z(o), f) for o in range(1, NZ)]
        + [(z * NQ + at_q(k), f) for k in range(1, NQ)]
    )

    def cot_copy():
        return remote(c, cx, xs.at[8], xr.at[8], d, other_x)

    def act_copy(block):
        columns = pl.ds(pl.multiple_of((1 - x) * HALF + block * SPAN, SPAN), SPAN)
        return remote(a.at[:, columns], ax.at[block], xs.at[block], xr.at[block], d, other_x)

    def own_piece(o):
        target = other_x if o == 0 else at_y(o)
        recv = wr.at[1, 0] if o == 0 else wr.at[0, o]
        return remote(w.at[piece], full.at[f, piece], ws.at[0, o], recv, d, target)

    def passed_piece(o):
        ref = full.at[other_x, piece]
        return remote(ref, ref, ws.at[1, o], wr.at[1, o], d, at_y(o))

    far_first = (4, 3, 5, 2, 6, 1, 7)
    own_piece(0).start()
    cot_copy().start()
    for o in far_first:
        own_piece(o).start()
    for o in (4, 3, -3, 2, -2, 1, -1, 0):
        act_copy(wrap_y(y + o)).start()

    local[0].wait()

    @pl.loop(0, SPAN // 32)
    def _(r):
        rows = pl.ds(pl.multiple_of(r * 32, 32), 32)
        level = lax.broadcasted_iota(jnp.int32, (32, KV), 0) + r * 32
        found = jnp.full((32, KV), -1, jnp.int32)
        for i in range(TOPK):
            row = jnp.broadcast_to(pos[i : i + 1, :], (32, KV))
            found = jnp.where(row == level, i, found)
        inv[rows, :] = found

    passed = full.at[other_x, piece]
    remote(w.at[piece], passed, ws.at[0, 0], wr.at[1, 0], d, other_x).wait_recv()
    for o in far_first:
        passed_piece(o).start()

    local[1].wait()
    local[2].wait()

    @pl.loop(0, NY)
    def _(block):
        columns = pl.ds(pl.multiple_of(block * SPAN, SPAN), SPAN)
        part[block] = lax.dot_general(av[:, columns], cv[...], TOKENS_IN, preferred_element_type=F32)

    def product(block):
        act_copy(block).wait_recv()
        part[block] += lax.dot_general(ax[block], cx[...], TOKENS_IN, preferred_element_type=F32)

    rows_of = SPAN // SUBS

    def half_copy(direction, sub):
        rows = pl.ds(sub * rows_of, rows_of)
        return remote(
            half_s.at[direction, rows], half_r.at[direction, rows], hs.at[direction, sub], hr.at[direction, sub],
            d, at_y(1 - 2 * direction),
        )

    def block_copy(direction, step, sub):
        rows = pl.ds(sub * rows_of, rows_of)
        return remote(
            block_s.at[direction, step, rows], block_r.at[direction, step, rows],
            ys.at[direction, step, sub], yr.at[direction, step, sub],
            d, at_y(1 - 2 * direction),
        )

    def send_halves():
        block = wrap_y(y + 4)
        for sub in range(SUBS):
            for direction in range(2):
                rows, columns = pl.ds(sub * rows_of, rows_of), pl.ds(direction * SPAN, SPAN)
                half_s[direction, rows] = part[block, rows, columns].astype(BF16)
                half_copy(direction, sub).start()

    def send_blocks(step):
        for sub in range(SUBS):
            for direction in range(2):
                rows = pl.ds(sub * rows_of, rows_of)
                block = wrap_y(y + (3 - step) * (1 - 2 * direction))
                if step == 0:
                    mine, others = pl.ds(direction * SPAN, SPAN), pl.ds((1 - direction) * SPAN, SPAN)
                    half_copy(direction, sub).wait_recv()
                    value = part[block, rows, mine] + half_r[direction, rows].astype(F32)
                    block_s[direction, step, rows, mine] = value.astype(BF16)
                    block_s[direction, step, rows, others] = part[block, rows, others].astype(BF16)
                else:
                    block_copy(direction, step - 1, sub).wait_recv()
                    value = part[block, rows, :] + block_r[direction, step - 1, rows].astype(F32)
                    block_s[direction, step, rows] = value.astype(BF16)
                block_copy(direction, step, sub).start()

    def z_block(direction, step, which):
        return wrap_z(z - step * (1 - 2 * direction)) * 2 + which

    def z_copy(direction, step, sub, arriving=0):
        ref = full.at[pl.ds(sub * 8, 8), z_block(direction, step + arriving, core)]
        return remote(
            ref, ref, zs.at[direction, step, sub], zr.at[direction, step, sub], at_z(1 - 2 * direction), f
        )

    def core_copy(direction, step, sub, which):
        ref = full.at[pl.ds(sub * 8, 8), z_block(direction, step, which)]
        return remote(ref, ref, cs.at[direction, step, sub], cr.at[direction, step, sub], other_core, f)

    def halves_of(direction, step):
        return (0, 1) if step < 3 else (direction,)

    forwards = [(0, 0, 0), (0, 0, 1)] + [
        (direction, step, sub)
        for step in range(1, 5)
        for direction in range(2)
        for sub in halves_of(direction, step - 1)
    ]

    def relay(step):
        for direction in range(2):
            for sub in halves_of(direction, step - 1):
                z_copy(direction, step - 1, sub, arriving=1).wait_recv()
                if step < 4 and sub in halves_of(direction, step):
                    z_copy(direction, step, sub).start()
                core_copy(direction, step, sub, core).start()

    cot_copy().wait_recv()
    product(wrap_y(y + 4))
    send_halves()
    for o in (3, -3):
        product(wrap_y(y + o))
    send_blocks(0)

    local[3].wait()
    for o in range(1, NY):
        ref = full.at[at_y(-o), piece]
        remote(ref, ref, ws.at[0, o], wr.at[0, o], d, at_y(o)).wait_recv()
        ref = full.at[lax.rem(at_y(-o) + NY, NX * NY), piece]
        remote(ref, ref, ws.at[1, o], wr.at[1, o], d, at_y(o)).wait_recv()
    for direction in range(2):
        for sub in range(2):
            z_copy(direction, 0, sub).start()
    for sub in range(2):
        core_copy(0, 0, sub, core).start()

    for o in (2, -2):
        product(wrap_y(y + o))
    send_blocks(1)
    relay(1)
    for o in (1, -1):
        product(wrap_y(y + o))
    send_blocks(2)
    relay(2)
    product(y)
    local[5].wait()
    for sub in range(SUBS):
        rows = pl.ds(sub * rows_of, rows_of)
        gradient = part[y, rows, :]
        for direction in range(2):
            block_copy(direction, 2, sub).wait_recv()
            gradient = gradient + block_r[direction, 2, rows].astype(F32)
        mv[rows, :] = MOMENTUM_DECAY * mv[rows, :] + gradient

    local[4].wait()
    coeffs[...] = dot_full(tv[...], mv[...], ((1,), (0,)))
    for column in range(KV // 128):
        lanes = pl.ds(column * 128, 128)
        picked = [
            pick_rows(coeffs[:, lanes], pos[pl.ds(r * 8, 8), lanes], SPAN // 8) for r in range(TOPK // 8)
        ]
        bands[:, lanes] = jnp.concatenate(picked, axis=0).astype(BF16)

    def one(k):
        columns = pl.ds(pl.multiple_of(at_q(k) * 128, 128), 128)
        return remote(bands.at[:, columns], first.at[k - 1], ss.at[0, k], sr.at[0, k], z * NQ + at_q(k), f)

    def two(o):
        return remote(total, second.at[z], ss.at[1, o], sr.at[1, o], at_z(o), f)

    def two_arrived(o):
        return remote(total, second.at[wrap_z(z - o)], ss.at[1, o], sr.at[1, o], at_z(o), f)

    def three(k):
        return remote(third.at[q], third.at[q], ss.at[2, k], sr.at[2, k], z * NQ + at_q(k), f)

    def three_arrived(k):
        slot = third.at[at_q(k)]
        return remote(slot, slot, ss.at[2, k], sr.at[2, k], z * NQ + at_q(k), f)

    def grad_inputs(low, high):
        @pl.loop(low, high)
        def _(tile):
            columns = pl.ds(pl.multiple_of(tile * 512, 512), 512)
            rows = full[pl.ds(tile * 2, 2)].reshape(512, KV)
            out[:, columns] = lax.dot_general(
                cv[...], rows, (((1,), (1,)), ((), ())), preferred_element_type=F32
            ).astype(BF16)

    for k in (3, 2, 1):
        one(k).start()
    relay(3)
    masked = jnp.where(inv[...] >= 0, coeffs[...], 0.0)
    kept[0] = mv[...] - dot_full(tv[...], masked, ((0,), (0,)))
    summed = bands[:, pl.ds(pl.multiple_of(q * 128, 128), 128)].astype(F32)
    for k in range(1, NQ):
        one(k).wait_recv()
        summed = summed + first[k - 1].astype(F32)
    total[...] = summed.astype(BF16)
    for o in far_first:
        two(o).start()
    second[z] = summed.astype(BF16)
    relay(4)
    for direction, step, sub in forwards:
        core_copy(direction, step, sub, 1 - core).wait_recv()
    grad_inputs(0, 5)
    for o in range(1, NZ):
        two_arrived(o).wait_recv()
    summed = second[0].astype(F32)
    for at in range(1, NZ):
        summed = summed + second[at].astype(F32)
    third[q] = summed / (NZ * NQ)
    for k in (3, 2, 1):
        three(k).start()
    grad_inputs(5, 8)
    for k in range(1, NQ):
        three_arrived(k).wait_recv()
    for at in range(NQ):
        mean[:, at * 128 : at * 128 + 128] = third[at]

    cot_copy().wait_send()
    for o in range(NY):
        act_copy(o).wait_send()
        own_piece(o).wait_send()
    for o in range(1, NY):
        passed_piece(o).wait_send()
    for direction in range(2):
        for sub in range(SUBS):
            half_copy(direction, sub).wait_send()
            for step in range(3):
                block_copy(direction, step, sub).wait_send()
        for step in range(4):
            for sub in halves_of(direction, step):
                z_copy(direction, step, sub).wait_send()
    for direction, step, sub in forwards:
        core_copy(direction, step, sub, core).wait_send()
    for k in range(1, NQ):
        one(k).wait_send()
        three(k).wait_send()
    for o in range(1, NZ):
        two(o).wait_send()


def step(activations, cotangent, weight, momentum, positions, table):
    hbm, vmem = pl.BlockSpec(memory_space=pltpu.HBM), pl.BlockSpec(memory_space=pltpu.VMEM)
    dma = pltpu.SemaphoreType.DMA
    return pl.pallas_call(
        step_kernel,
        out_shape=(
            jax.ShapeDtypeStruct((1, SPAN, KV), F32),
            jax.ShapeDtypeStruct((TOK, FEAT), BF16),
            jax.ShapeDtypeStruct((TOPK, KV), F32),
            jax.ShapeDtypeStruct((SPAN, KV), jnp.int32),
        ),
        in_specs=[hbm] * 6,
        out_specs=(vmem,) * 4,
        scratch_shapes=[
            pltpu.VMEM((TOK, HALF), BF16),
            pltpu.VMEM((TOK, KV), BF16),
            pltpu.VMEM((TOPK, KV), jnp.int32),
            pltpu.VMEM((SPAN, SPAN), F32),
            pltpu.VMEM((SPAN, KV), F32),
            pltpu.VMEM((NY, TOK, SPAN), BF16),
            pltpu.VMEM((TOK, KV), BF16),
            pltpu.VMEM((NY, SPAN, KV), F32),
            pltpu.VMEM((16, 16, 16, KV), BF16),
            pltpu.VMEM((2, SPAN, SPAN), BF16),
            pltpu.VMEM((2, SPAN, SPAN), BF16),
            pltpu.VMEM((2, 3, SPAN, KV), BF16),
            pltpu.VMEM((2, 3, SPAN, KV), BF16),
            pltpu.VMEM((SPAN, KV), F32),
            pltpu.VMEM((TOPK, KV), BF16),
            pltpu.VMEM((3, TOPK, 128), BF16),
            pltpu.VMEM((TOPK, 128), BF16),
            pltpu.VMEM((NZ, TOPK, 128), BF16),
            pltpu.VMEM((NQ, TOPK, 128), F32),
            dma((6,)),
            dma((9,)), dma((9,)),
            dma((2, SUBS)), dma((2, SUBS)),
            dma((2, 3, SUBS)), dma((2, 3, SUBS)),
            dma((2, NY)), dma((2, NY)),
            dma((2, 4, 2)), dma((2, 4, 2)),
            dma((2, 5, 2)), dma((2, 5, 2)),
            dma((3, 8)), dma((3, 8)),
        ],
        compiler_params=pltpu.CompilerParams(
            collective_id=0, has_side_effects=True, vmem_limit_bytes=40 << 20
        ),
        name="step",
    )(activations, cotangent, weight, momentum, positions, table)


def finish_kernel(table, mean, inv, given, moment, update, result, kept, dense, sem):
    copies = [pltpu.make_async_copy(given, result, sem.at[0]), pltpu.make_async_copy(moment, kept, sem.at[1])]
    for copy in copies:
        copy.start()
    for column in range(KV // 128):
        lanes = pl.ds(column * 128, 128)
        for r in range(SPAN // 8):
            dense[pl.ds(r * 8, 8), lanes] = pick_rows(mean[:, lanes], inv[pl.ds(r * 8, 8), lanes], TOPK // 8)
    update[...] = dot_full(table[...], dense[...], ((0,), (0,))).astype(BF16)
    for copy in copies:
        copy.wait()


def finish(table, mean, inv, given, moment):
    hbm, vmem = pl.BlockSpec(memory_space=pltpu.HBM), pl.BlockSpec(memory_space=pltpu.VMEM)
    return pl.pallas_call(
        finish_kernel,
        out_shape=(
            jax.ShapeDtypeStruct((SPAN, KV), BF16),
            jax.ShapeDtypeStruct((TOK, FEAT), BF16),
            jax.ShapeDtypeStruct((1, SPAN, KV), F32),
        ),
        in_specs=[vmem] * 5,
        out_specs=(vmem, hbm, hbm),
        scratch_shapes=[pltpu.VMEM((SPAN, KV), F32), pltpu.SemaphoreType.DMA((2,))],
        compiler_params=pltpu.CompilerParams(vmem_limit_bytes=8 << 20),
        name="finish",
    )(table, mean, inv, given, moment)


def on_device(activations, cotangent, weight, momentum, positions):
    table = jnp.asarray(transform_table(SPAN))
    held = [
        pltpu.with_memory_space_constraint(array, pltpu.HBM)
        for array in (activations, cotangent, weight.reshape(16, 16, KV), momentum[0], positions[0], table)
    ]
    moment, product, mean, inv = step(*held)
    update, grad_input, kept = finish(table, mean, inv, product, moment)
    return grad_input, kept, update


def solution(mesh):
    placed = (
        P(("dp", "fsdp"), None),
        P(("dp", "fsdp"), None),
        P("fsdp", None),
        P("dp", "fsdp", None),
        P("fsdp", None, None),
    )
    return jax.shard_map(
        on_device,
        mesh=mesh,
        in_specs=placed,
        out_specs=(P(("dp", "fsdp"), None), P("dp", "fsdp", None), P("fsdp", None)),
        check_vma=False,
    )
```

```python
import functools

import jax
import jax.numpy as jnp
import numpy as np
from jax import lax
from jax.experimental import pallas as pl
from jax.experimental.pallas import tpu as pltpu
from jax.sharding import PartitionSpec as P

NZ, NQ, NX, NY = 8, 4, 2, 8
SPAN, KV, TOPK, TOK, FEAT = 256, 512, 32, 192, 4096
HALF = FEAT // NX
SUBS = 4
TOKENS_IN = (((0,), (0,)), ((), ()))
MOMENTUM_DECAY = 0.999
MESH = pl.DeviceIdType.MESH
F32, BF16 = jnp.float32, jnp.bfloat16


def transform_table(length):
    freq = np.arange(length, dtype=np.float64)[:, None]
    place = np.arange(length, dtype=np.float64)[None, :]
    scales = np.where(freq == 0, np.sqrt(1.0 / length), np.sqrt(2.0 / length))
    return (scales * np.cos(np.pi * (2 * place + 1) * freq / (2 * length))).astype(np.float32)


def remote(src, dst, send, recv, dp, fsdp):
    return pltpu.make_async_remote_copy(
        src_ref=src, dst_ref=dst, send_sem=send, recv_sem=recv,
        device_id=(dp, fsdp), device_id_type=MESH,
    )


def meet(peers):
    barrier = pltpu.get_barrier_semaphore()
    for peer in peers:
        pl.semaphore_signal(barrier, inc=1, device_id=peer, device_id_type=MESH)
    pl.semaphore_wait(barrier, len(peers))


def pick_rows(values, where, groups):
    low, high = where & 7, where >> 3
    found = jnp.zeros(where.shape, values.dtype)
    for group in range(groups):
        rows = jnp.take_along_axis(values[group * 8 : group * 8 + 8, :], low, axis=0)
        found = jnp.where(high == group, rows, found)
    return found


def dot_full(left, right, dims):
    return lax.dot_general(
        left, right, (dims, ((), ())), precision=lax.Precision.HIGHEST, preferred_element_type=F32
    )


def step_kernel(
    a, c, w, momentum, positions, table,
    kept, out, mean, inv,
    av, cv, pos, tv, mv, ax, cx, part, full, half_s, half_r, block_s, block_r,
    coeffs, bands, first, total, second, third,
    ls, xs, xr, hs, hr, ys, yr, ws, wr, zs, zr, fs, fr, cs, cr, ss, sr,
):
    d, f = lax.axis_index("dp"), lax.axis_index("fsdp")
    x, y = f // NY, lax.rem(f, NY)
    z, q = d // NQ, lax.rem(d, NQ)
    hi, core = q // 2, lax.rem(q, 2)
    piece = z * 2 + core
    other_x = lax.rem(f + NY, NX * NY)
    other_core = d + 1 - 2 * core
    other_hi = z * NQ + (1 - hi) * 2 + core

    def wrap_y(at):
        return lax.rem(at + 2 * NY, NY)

    def wrap_z(at):
        return lax.rem(at + 2 * NZ, NZ)

    def at_y(step):
        return x * NY + wrap_y(y + step)

    def at_z(step):
        return wrap_z(z + step) * NQ + q

    def at_q(k):
        new_hi = 1 - hi if k // 2 else hi
        new_core = 1 - core if k % 2 else core
        return new_hi * 2 + new_core

    local = [
        pltpu.make_async_copy(positions, pos, ls.at[0]),
        pltpu.make_async_copy(c, cv, ls.at[1]),
        pltpu.make_async_copy(a.at[:, pl.ds(pl.multiple_of(x * HALF, HALF), HALF)], av, ls.at[2]),
        pltpu.make_async_copy(w.at[piece], full.at[f, piece], ls.at[3]),
        pltpu.make_async_copy(table, tv, ls.at[4]),
        pltpu.make_async_copy(momentum, mv, ls.at[5]),
    ]
    for copy in local:
        copy.start()

    meet(
        [(d, other_x), (other_hi, other_x), (d, at_y(1)), (d, at_y(-1)), (at_z(1), f), (at_z(-1), f)]
        + [(z * NQ + at_q(k), f) for k in range(1, NQ)]
    )

    def cot_copy():
        return remote(c, cx, xs.at[8], xr.at[8], d, other_x)

    def act_copy(block):
        columns = pl.ds(pl.multiple_of((1 - x) * HALF + block * SPAN, SPAN), SPAN)
        return remote(a.at[:, columns], ax.at[block], xs.at[block], xr.at[block], d, other_x)

    def piece_copy(direction, step, arriving=0):
        way = 1 - 2 * direction
        ref = full.at[at_y(-(step + arriving) * way), piece]
        first_hop = step == 0 and not arriving
        return remote(
            w.at[piece] if first_hop else ref, ref, ws.at[direction, step], wr.at[direction, step], d, at_y(way)
        )

    def pass_pieces(step):
        for direction in range(2):
            if step - 1 < 4 - direction:
                piece_copy(direction, step - 1, arriving=1).wait_recv()
            if step < 4 - direction:
                piece_copy(direction, step).start()

    far_first = (4, 3, 5, 2, 6, 1, 7)
    for direction in range(2):
        piece_copy(direction, 0).start()
    cot_copy().start()
    for o in (4, 3, -3, 2, -2, 1, -1, 0):
        act_copy(wrap_y(y + o)).start()

    local[0].wait()

    @pl.loop(0, SPAN // 32)
    def _(r):
        rows = pl.ds(pl.multiple_of(r * 32, 32), 32)
        level = lax.broadcasted_iota(jnp.int32, (32, KV), 0) + r * 32
        found = jnp.full((32, KV), -1, jnp.int32)
        for i in range(TOPK):
            row = jnp.broadcast_to(pos[i : i + 1, :], (32, KV))
            found = jnp.where(row == level, i, found)
        inv[rows, :] = found

    pass_pieces(1)

    local[1].wait()
    local[2].wait()

    @pl.loop(0, NY)
    def _(block):
        columns = pl.ds(pl.multiple_of(block * SPAN, SPAN), SPAN)
        part[block] = lax.dot_general(av[:, columns], cv[...], TOKENS_IN, preferred_element_type=F32)

    pass_pieces(2)

    def product(block):
        act_copy(block).wait_recv()
        part[block] += lax.dot_general(ax[block], cx[...], TOKENS_IN, preferred_element_type=F32)

    rows_of = SPAN // SUBS

    def half_copy(direction, sub):
        rows = pl.ds(sub * rows_of, rows_of)
        return remote(
            half_s.at[direction, rows], half_r.at[direction, rows], hs.at[direction, sub], hr.at[direction, sub],
            d, at_y(1 - 2 * direction),
        )

    def block_copy(direction, step, sub):
        rows = pl.ds(sub * rows_of, rows_of)
        return remote(
            block_s.at[direction, step, rows], block_r.at[direction, step, rows],
            ys.at[direction, step, sub], yr.at[direction, step, sub],
            d, at_y(1 - 2 * direction),
        )

    def send_halves():
        block = wrap_y(y + 4)
        for sub in range(SUBS):
            for direction in range(2):
                rows, columns = pl.ds(sub * rows_of, rows_of), pl.ds(direction * SPAN, SPAN)
                half_s[direction, rows] = part[block, rows, columns].astype(BF16)
                half_copy(direction, sub).start()

    def send_blocks(step):
        for sub in range(SUBS):
            for direction in range(2):
                rows = pl.ds(sub * rows_of, rows_of)
                block = wrap_y(y + (3 - step) * (1 - 2 * direction))
                if step == 0:
                    mine, others = pl.ds(direction * SPAN, SPAN), pl.ds((1 - direction) * SPAN, SPAN)
                    half_copy(direction, sub).wait_recv()
                    value = part[block, rows, mine] + half_r[direction, rows].astype(F32)
                    block_s[direction, step, rows, mine] = value.astype(BF16)
                    block_s[direction, step, rows, others] = part[block, rows, others].astype(BF16)
                else:
                    block_copy(direction, step - 1, sub).wait_recv()
                    value = part[block, rows, :] + block_r[direction, step - 1, rows].astype(F32)
                    block_s[direction, step, rows] = value.astype(BF16)
                block_copy(direction, step, sub).start()

    def z_block(direction, step, which):
        return wrap_z(z - step * (1 - 2 * direction)) * 2 + which

    def shards(side, sub):
        return pl.ds(side * 8 + sub * 4, 4)

    def z_copy(direction, step, sub, arriving=0):
        ref = full.at[shards(x, sub), z_block(direction, step + arriving, core)]
        return remote(
            ref, ref, zs.at[direction, step, sub], zr.at[direction, step, sub], at_z(1 - 2 * direction), f
        )

    def far_copy(direction, step, sub, side):
        ref = full.at[shards(side, sub), z_block(direction, step, core)]
        return remote(
            ref, ref, fs.at[direction, step, sub], fr.at[direction, step, sub], other_hi, other_x
        )

    def core_copy(far, direction, step, sub, which):
        side = 1 - x if far else x
        ref = full.at[shards(side, sub), z_block(direction, step, which)]
        return remote(
            ref, ref, cs.at[far, direction, step, sub], cr.at[far, direction, step, sub], other_core, f
        )

    def units(step):
        if step == 0:
            return ((0, 0), (0, 1))
        if step == 4:
            return ((0, 0), (1, 1))
        return ((0, 0), (1, 0), (0, 1), (1, 1))

    def relay(step):
        if step == 0:
            for sub in range(2):
                for direction in range(2):
                    z_copy(direction, 0, sub).start()
        elif step < 5:
            for direction, sub in units(step):
                z_copy(direction, step - 1, sub, arriving=1).wait_recv()
                if step < 3 or (step == 3 and sub == direction):
                    z_copy(direction, step, sub).start()
        if step < 5:
            for direction, sub in units(step):
                far_copy(direction, step, sub, x).start()
                core_copy(0, direction, step, sub, core).start()
        if step > 0:
            for direction, sub in units(step - 1):
                far_copy(direction, step - 1, sub, 1 - x).wait_recv()
                core_copy(1, direction, step - 1, sub, core).start()

    pass_pieces(3)
    cot_copy().wait_recv()
    product(wrap_y(y + 4))
    send_halves()
    local[3].wait()
    pass_pieces(4)
    relay(0)
    for o in (3, -3):
        product(wrap_y(y + o))
    send_blocks(0)
    relay(1)
    for o in (2, -2):
        product(wrap_y(y + o))
    send_blocks(1)
    relay(2)
    for o in (1, -1):
        product(wrap_y(y + o))
    send_blocks(2)
    relay(3)
    product(y)
    local[5].wait()
    for sub in range(SUBS):
        rows = pl.ds(sub * rows_of, rows_of)
        gradient = part[y, rows, :]
        for direction in range(2):
            block_copy(direction, 2, sub).wait_recv()
            gradient = gradient + block_r[direction, 2, rows].astype(F32)
        mv[rows, :] = MOMENTUM_DECAY * mv[rows, :] + gradient

    local[4].wait()
    coeffs[...] = dot_full(tv[...], mv[...], ((1,), (0,)))
    for column in range(KV // 128):
        lanes = pl.ds(column * 128, 128)
        picked = [
            pick_rows(coeffs[:, lanes], pos[pl.ds(r * 8, 8), lanes], SPAN // 8) for r in range(TOPK // 8)
        ]
        bands[:, lanes] = jnp.concatenate(picked, axis=0).astype(BF16)

    def one(k):
        columns = pl.ds(pl.multiple_of(at_q(k) * 128, 128), 128)
        return remote(bands.at[:, columns], first.at[k - 1], ss.at[0, k], sr.at[0, k], z * NQ + at_q(k), f)

    def two(o):
        return remote(total, second.at[z], ss.at[1, o], sr.at[1, o], at_z(o), f)

    def two_arrived(o):
        return remote(total, second.at[wrap_z(z - o)], ss.at[1, o], sr.at[1, o], at_z(o), f)

    def three(k):
        return remote(third.at[q], third.at[q], ss.at[2, k], sr.at[2, k], z * NQ + at_q(k), f)

    def three_arrived(k):
        slot = third.at[at_q(k)]
        return remote(slot, slot, ss.at[2, k], sr.at[2, k], z * NQ + at_q(k), f)

    def grad_inputs(low, high):
        @pl.loop(low, high)
        def _(tile):
            columns = pl.ds(pl.multiple_of(tile * 512, 512), 512)
            rows = full[pl.ds(tile * 2, 2)].reshape(512, KV)
            out[:, columns] = lax.dot_general(
                cv[...], rows, (((1,), (1,)), ((), ())), preferred_element_type=F32
            ).astype(BF16)

    forwards = [(far, way, step, sub) for step in range(5) for far in range(2) for way, sub in units(step)]
    for k in (3, 2, 1):
        one(k).start()
    relay(4)
    masked = jnp.where(inv[...] >= 0, coeffs[...], 0.0)
    kept[0] = mv[...] - dot_full(tv[...], masked, ((0,), (0,)))
    summed = bands[:, pl.ds(pl.multiple_of(q * 128, 128), 128)].astype(F32)
    for k in range(1, NQ):
        one(k).wait_recv()
        summed = summed + first[k - 1].astype(F32)
    total[...] = summed.astype(BF16)
    for o in far_first:
        two(o).start()
    second[z] = summed.astype(BF16)
    relay(5)
    for far, direction, step, sub in forwards:
        core_copy(far, direction, step, sub, 1 - core).wait_recv()
    grad_inputs(0, 5)
    for o in range(1, NZ):
        two_arrived(o).wait_recv()
    summed = second[0].astype(F32)
    for at in range(1, NZ):
        summed = summed + second[at].astype(F32)
    third[q] = summed / (NZ * NQ)
    for k in (3, 2, 1):
        three(k).start()
    grad_inputs(5, 8)
    for k in range(1, NQ):
        three_arrived(k).wait_recv()
    for at in range(NQ):
        mean[:, at * 128 : at * 128 + 128] = third[at]

    cot_copy().wait_send()
    for o in range(NY):
        act_copy(o).wait_send()
    for direction in range(2):
        for sub in range(SUBS):
            half_copy(direction, sub).wait_send()
            for step in range(3):
                block_copy(direction, step, sub).wait_send()
        for step in range(4):
            if step < 4 - direction:
                piece_copy(direction, step).wait_send()
            for sub in range(2):
                if step < 3 or sub == direction:
                    z_copy(direction, step, sub).wait_send()
    for far, direction, step, sub in forwards:
        core_copy(far, direction, step, sub, core).wait_send()
        if far:
            far_copy(direction, step, sub, x).wait_send()
    for k in range(1, NQ):
        one(k).wait_send()
        three(k).wait_send()
    for o in range(1, NZ):
        two(o).wait_send()


def step(activations, cotangent, weight, momentum, positions, table):
    hbm, vmem = pl.BlockSpec(memory_space=pltpu.HBM), pl.BlockSpec(memory_space=pltpu.VMEM)
    dma = pltpu.SemaphoreType.DMA
    return pl.pallas_call(
        step_kernel,
        out_shape=(
            jax.ShapeDtypeStruct((1, SPAN, KV), F32),
            jax.ShapeDtypeStruct((TOK, FEAT), BF16),
            jax.ShapeDtypeStruct((TOPK, KV), F32),
            jax.ShapeDtypeStruct((SPAN, KV), jnp.int32),
        ),
        in_specs=[hbm] * 6,
        out_specs=(vmem,) * 4,
        scratch_shapes=[
            pltpu.VMEM((TOK, HALF), BF16),
            pltpu.VMEM((TOK, KV), BF16),
            pltpu.VMEM((TOPK, KV), jnp.int32),
            pltpu.VMEM((SPAN, SPAN), F32),
            pltpu.VMEM((SPAN, KV), F32),
            pltpu.VMEM((NY, TOK, SPAN), BF16),
            pltpu.VMEM((TOK, KV), BF16),
            pltpu.VMEM((NY, SPAN, KV), F32),
            pltpu.VMEM((16, 16, 16, KV), BF16),
            pltpu.VMEM((2, SPAN, SPAN), BF16),
            pltpu.VMEM((2, SPAN, SPAN), BF16),
            pltpu.VMEM((2, 3, SPAN, KV), BF16),
            pltpu.VMEM((2, 3, SPAN, KV), BF16),
            pltpu.VMEM((SPAN, KV), F32),
            pltpu.VMEM((TOPK, KV), BF16),
            pltpu.VMEM((3, TOPK, 128), BF16),
            pltpu.VMEM((TOPK, 128), BF16),
            pltpu.VMEM((NZ, TOPK, 128), BF16),
            pltpu.VMEM((NQ, TOPK, 128), F32),
            dma((6,)),
            dma((9,)), dma((9,)),
            dma((2, SUBS)), dma((2, SUBS)),
            dma((2, 3, SUBS)), dma((2, 3, SUBS)),
            dma((2, 4)), dma((2, 4)),
            dma((2, 4, 2)), dma((2, 4, 2)),
            dma((2, 5, 2)), dma((2, 5, 2)),
            dma((2, 2, 5, 2)), dma((2, 2, 5, 2)),
            dma((3, 8)), dma((3, 8)),
        ],
        compiler_params=pltpu.CompilerParams(
            collective_id=0, has_side_effects=True, vmem_limit_bytes=40 << 20
        ),
        name="step",
    )(activations, cotangent, weight, momentum, positions, table)


def finish_kernel(table, mean, inv, given, moment, update, result, kept, dense, sem):
    copies = [pltpu.make_async_copy(given, result, sem.at[0]), pltpu.make_async_copy(moment, kept, sem.at[1])]
    for copy in copies:
        copy.start()
    for column in range(KV // 128):
        lanes = pl.ds(column * 128, 128)
        for r in range(SPAN // 8):
            dense[pl.ds(r * 8, 8), lanes] = pick_rows(mean[:, lanes], inv[pl.ds(r * 8, 8), lanes], TOPK // 8)
    update[...] = dot_full(table[...], dense[...], ((0,), (0,))).astype(BF16)
    for copy in copies:
        copy.wait()


def finish(table, mean, inv, given, moment):
    hbm, vmem = pl.BlockSpec(memory_space=pltpu.HBM), pl.BlockSpec(memory_space=pltpu.VMEM)
    return pl.pallas_call(
        finish_kernel,
        out_shape=(
            jax.ShapeDtypeStruct((SPAN, KV), BF16),
            jax.ShapeDtypeStruct((TOK, FEAT), BF16),
            jax.ShapeDtypeStruct((1, SPAN, KV), F32),
        ),
        in_specs=[vmem] * 5,
        out_specs=(vmem, hbm, hbm),
        scratch_shapes=[pltpu.VMEM((SPAN, KV), F32), pltpu.SemaphoreType.DMA((2,))],
        compiler_params=pltpu.CompilerParams(vmem_limit_bytes=8 << 20),
        name="finish",
    )(table, mean, inv, given, moment)


def on_device(activations, cotangent, weight, momentum, positions):
    table = jnp.asarray(transform_table(SPAN))
    held = [
        pltpu.with_memory_space_constraint(array, pltpu.HBM)
        for array in (activations, cotangent, weight.reshape(16, 16, KV), momentum[0], positions[0], table)
    ]
    moment, product, mean, inv = step(*held)
    update, grad_input, kept = finish(table, mean, inv, product, moment)
    return grad_input, kept, update


def solution(mesh):
    placed = (
        P(("dp", "fsdp"), None),
        P(("dp", "fsdp"), None),
        P("fsdp", None),
        P("dp", "fsdp", None),
        P("fsdp", None, None),
    )
    return jax.shard_map(
        on_device,
        mesh=mesh,
        in_specs=placed,
        out_specs=(P(("dp", "fsdp"), None), P("dp", "fsdp", None), P("fsdp", None)),
        check_vma=False,
    )
```

```python
import functools

import jax
import jax.numpy as jnp
import numpy as np
from jax import lax
from jax.experimental import pallas as pl
from jax.experimental.pallas import tpu as pltpu
from jax.sharding import PartitionSpec as P

NZ, NQ, NX, NY = 8, 4, 2, 8
SPAN, KV, TOPK, TOK, FEAT = 256, 512, 32, 192, 4096
HALF = FEAT // NX
SUBS = 4
TOKENS_IN = (((0,), (0,)), ((), ()))
MOMENTUM_DECAY = 0.999
MESH = pl.DeviceIdType.MESH
F32, BF16 = jnp.float32, jnp.bfloat16


def transform_table(length):
    freq = np.arange(length, dtype=np.float64)[:, None]
    place = np.arange(length, dtype=np.float64)[None, :]
    scales = np.where(freq == 0, np.sqrt(1.0 / length), np.sqrt(2.0 / length))
    return (scales * np.cos(np.pi * (2 * place + 1) * freq / (2 * length))).astype(np.float32)


def remote(src, dst, send, recv, dp, fsdp):
    return pltpu.make_async_remote_copy(
        src_ref=src, dst_ref=dst, send_sem=send, recv_sem=recv,
        device_id=(dp, fsdp), device_id_type=MESH,
    )


def meet(peers):
    barrier = pltpu.get_barrier_semaphore()
    for peer in peers:
        pl.semaphore_signal(barrier, inc=1, device_id=peer, device_id_type=MESH)
    pl.semaphore_wait(barrier, len(peers))


def pick_rows(values, where, groups):
    low, high = where & 7, where >> 3
    found = jnp.zeros(where.shape, values.dtype)
    for group in range(groups):
        rows = jnp.take_along_axis(values[group * 8 : group * 8 + 8, :], low, axis=0)
        found = jnp.where(high == group, rows, found)
    return found


def dot_full(left, right, dims):
    return lax.dot_general(
        left, right, (dims, ((), ())), precision=lax.Precision.HIGHEST, preferred_element_type=F32
    )


def step_kernel(
    a, c, w, momentum, positions, table,
    kept, out, mean, inv,
    av, cv, pos, tv, mv, ax, cx, part, full, half_s, half_r, block_s, block_r,
    coeffs, bands, first, total, second, third,
    ls, xs, xr, hs, hr, ys, yr, ws, wr, zs, zr, fs, fr, cs, cr, ss, sr,
):
    d, f = lax.axis_index("dp"), lax.axis_index("fsdp")
    x, y = f // NY, lax.rem(f, NY)
    z, q = d // NQ, lax.rem(d, NQ)
    hi, core = q // 2, lax.rem(q, 2)
    piece = z * 2 + core
    other_x = lax.rem(f + NY, NX * NY)
    other_core = d + 1 - 2 * core
    other_hi = z * NQ + (1 - hi) * 2 + core

    def wrap_y(at):
        return lax.rem(at + 2 * NY, NY)

    def wrap_z(at):
        return lax.rem(at + 2 * NZ, NZ)

    def at_y(step):
        return x * NY + wrap_y(y + step)

    def at_z(step):
        return wrap_z(z + step) * NQ + q

    def at_q(k):
        new_hi = 1 - hi if k // 2 else hi
        new_core = 1 - core if k % 2 else core
        return new_hi * 2 + new_core

    local = [
        pltpu.make_async_copy(positions, pos, ls.at[0]),
        pltpu.make_async_copy(c, cv, ls.at[1]),
        pltpu.make_async_copy(a.at[:, pl.ds(pl.multiple_of(x * HALF, HALF), HALF)], av, ls.at[2]),
        pltpu.make_async_copy(w.at[piece], full.at[f, piece], ls.at[3]),
        pltpu.make_async_copy(table, tv, ls.at[4]),
        pltpu.make_async_copy(momentum, mv, ls.at[5]),
    ]
    for copy in local:
        copy.start()

    meet(
        [(d, other_x), (other_hi, other_x), (d, at_y(1)), (d, at_y(-1)), (at_z(1), f), (at_z(-1), f)]
        + [(z * NQ + at_q(k), f) for k in range(1, NQ)]
    )

    def cot_copy():
        return remote(c, cx, xs.at[8], xr.at[8], d, other_x)

    def act_copy(block):
        columns = pl.ds(pl.multiple_of((1 - x) * HALF + block * SPAN, SPAN), SPAN)
        return remote(a.at[:, columns], ax.at[block], xs.at[block], xr.at[block], d, other_x)

    def piece_copy(direction, step, arriving=0):
        way = 1 - 2 * direction
        ref = full.at[at_y(-(step + arriving) * way), piece]
        first_hop = step == 0 and not arriving
        return remote(
            w.at[piece] if first_hop else ref, ref, ws.at[direction, step], wr.at[direction, step], d, at_y(way)
        )

    def pass_pieces(step):
        for direction in range(2):
            if step - 1 < 4 - direction:
                piece_copy(direction, step - 1, arriving=1).wait_recv()
            if step < 4 - direction:
                piece_copy(direction, step).start()

    far_first = (4, 3, 5, 2, 6, 1, 7)
    for direction in range(2):
        piece_copy(direction, 0).start()
    cot_copy().start()
    for o in (4, 3, -3, 2, -2, 1, -1, 0):
        act_copy(wrap_y(y + o)).start()

    local[0].wait()

    @pl.loop(0, SPAN // 32)
    def _(r):
        rows = pl.ds(pl.multiple_of(r * 32, 32), 32)
        level = lax.broadcasted_iota(jnp.int32, (32, KV), 0) + r * 32
        found = jnp.full((32, KV), -1, jnp.int32)
        for i in range(TOPK):
            row = jnp.broadcast_to(pos[i : i + 1, :], (32, KV))
            found = jnp.where(row == level, i, found)
        inv[rows, :] = found

    pass_pieces(1)

    local[1].wait()
    local[2].wait()

    @pl.loop(0, NY)
    def _(block):
        columns = pl.ds(pl.multiple_of(block * SPAN, SPAN), SPAN)
        part[block] = lax.dot_general(av[:, columns], cv[...], TOKENS_IN, preferred_element_type=F32)

    pass_pieces(2)

    def product(block):
        act_copy(block).wait_recv()
        part[block] += lax.dot_general(ax[block], cx[...], TOKENS_IN, preferred_element_type=F32)

    rows_of = SPAN // SUBS

    def half_copy(direction, sub):
        rows = pl.ds(sub * rows_of, rows_of)
        return remote(
            half_s.at[direction, rows], half_r.at[direction, rows], hs.at[direction, sub], hr.at[direction, sub],
            d, at_y(1 - 2 * direction),
        )

    def block_copy(direction, step, sub):
        rows = pl.ds(sub * rows_of, rows_of)
        return remote(
            block_s.at[direction, step, rows], block_r.at[direction, step, rows],
            ys.at[direction, step, sub], yr.at[direction, step, sub],
            d, at_y(1 - 2 * direction),
        )

    def send_halves():
        block = wrap_y(y + 4)
        for sub in range(SUBS):
            for direction in range(2):
                rows, columns = pl.ds(sub * rows_of, rows_of), pl.ds(direction * SPAN, SPAN)
                half_s[direction, rows] = part[block, rows, columns].astype(BF16)
                half_copy(direction, sub).start()

    def send_blocks(step):
        for sub in range(SUBS):
            for direction in range(2):
                rows = pl.ds(sub * rows_of, rows_of)
                block = wrap_y(y + (3 - step) * (1 - 2 * direction))
                if step == 0:
                    mine, others = pl.ds(direction * SPAN, SPAN), pl.ds((1 - direction) * SPAN, SPAN)
                    half_copy(direction, sub).wait_recv()
                    value = part[block, rows, mine] + half_r[direction, rows].astype(F32)
                    block_s[direction, step, rows, mine] = value.astype(BF16)
                    block_s[direction, step, rows, others] = part[block, rows, others].astype(BF16)
                else:
                    block_copy(direction, step - 1, sub).wait_recv()
                    value = part[block, rows, :] + block_r[direction, step - 1, rows].astype(F32)
                    block_s[direction, step, rows] = value.astype(BF16)
                block_copy(direction, step, sub).start()

    def z_block(direction, step, which):
        return wrap_z(z - step * (1 - 2 * direction)) * 2 + which

    def shards(side, sub):
        return pl.ds(side * 8 + sub * 4, 4)

    def z_copy(direction, step, sub, arriving=0):
        ref = full.at[shards(x, sub), z_block(direction, step + arriving, core)]
        return remote(
            ref, ref, zs.at[direction, step, sub], zr.at[direction, step, sub], at_z(1 - 2 * direction), f
        )

    def far_copy(direction, step, sub, side):
        ref = full.at[shards(side, sub), z_block(direction, step, core)]
        return remote(
            ref, ref, fs.at[direction, step, sub], fr.at[direction, step, sub], other_hi, other_x
        )

    def core_copy(far, direction, step, sub, which):
        side = 1 - x if far else x
        ref = full.at[shards(side, sub), z_block(direction, step, which)]
        return remote(
            ref, ref, cs.at[far, direction, step, sub], cr.at[far, direction, step, sub], other_core, f
        )

    def units(step):
        if step == 0:
            return ((0, 0), (0, 1))
        if step == 4:
            return ((0, 0), (1, 1))
        return ((0, 0), (1, 0), (0, 1), (1, 1))

    def relay(step):
        if step == 0:
            for sub in range(2):
                for direction in range(2):
                    z_copy(direction, 0, sub).start()
        elif step < 5:
            for direction, sub in units(step):
                z_copy(direction, step - 1, sub, arriving=1).wait_recv()
                if step < 3 or (step == 3 and sub == direction):
                    z_copy(direction, step, sub).start()
        if step < 5:
            for direction, sub in units(step):
                far_copy(direction, step, sub, x).start()
                core_copy(0, direction, step, sub, core).start()
        if step > 0:
            for direction, sub in units(step - 1):
                far_copy(direction, step - 1, sub, 1 - x).wait_recv()
                core_copy(1, direction, step - 1, sub, core).start()

    pass_pieces(3)
    cot_copy().wait_recv()
    product(wrap_y(y + 4))
    send_halves()
    local[3].wait()
    pass_pieces(4)
    relay(0)
    for o in (3, -3):
        product(wrap_y(y + o))
    send_blocks(0)
    relay(1)
    for o in (2, -2):
        product(wrap_y(y + o))
    send_blocks(1)
    relay(2)
    for o in (1, -1):
        product(wrap_y(y + o))
    send_blocks(2)
    relay(3)
    product(y)
    local[5].wait()
    mv[...] = MOMENTUM_DECAY * mv[...] + part[y]
    for sub in range(SUBS):
        rows = pl.ds(sub * rows_of, rows_of)
        moment = mv[rows, :]
        for direction in range(2):
            block_copy(direction, 2, sub).wait_recv()
            moment = moment + block_r[direction, 2, rows].astype(F32)
        mv[rows, :] = moment

    def one(k):
        columns = pl.ds(pl.multiple_of(at_q(k) * 128, 128), 128)
        return remote(bands.at[:, columns], first.at[k - 1], ss.at[0, k], sr.at[0, k], z * NQ + at_q(k), f)

    def two(o):
        return remote(total, second.at[z], ss.at[1, o], sr.at[1, o], at_z(o), f)

    def two_arrived(o):
        return remote(total, second.at[wrap_z(z - o)], ss.at[1, o], sr.at[1, o], at_z(o), f)

    def three(k):
        return remote(third.at[q], third.at[q], ss.at[2, k], sr.at[2, k], z * NQ + at_q(k), f)

    def three_arrived(k):
        slot = third.at[at_q(k)]
        return remote(slot, slot, ss.at[2, k], sr.at[2, k], z * NQ + at_q(k), f)

    def grad_inputs(side):
        @pl.loop(0, 4)
        def _(at):
            tile = side * 4 + at
            columns = pl.ds(pl.multiple_of(tile * 512, 512), 512)
            rows = full[pl.ds(tile * 2, 2)].reshape(512, KV)
            out[:, columns] = lax.dot_general(
                cv[...], rows, (((1,), (1,)), ((), ())), preferred_element_type=F32
            ).astype(BF16)

    forwards = [(far, way, step, sub) for step in range(5) for far in range(2) for way, sub in units(step)]
    local[4].wait()
    for to in ((3, 2), (1, 0)):
        side = pl.ds(pl.multiple_of(at_q(to[1]) // 2 * SPAN, SPAN), SPAN)
        coeffs[:, side] = dot_full(tv[...], mv[:, side], ((1,), (0,)))
        for k in to:
            lanes = pl.ds(pl.multiple_of(at_q(k) * 128, 128), 128)
            picked = [
                pick_rows(coeffs[:, lanes], pos[pl.ds(r * 8, 8), lanes], SPAN // 8) for r in range(TOPK // 8)
            ]
            bands[:, lanes] = jnp.concatenate(picked, axis=0).astype(BF16)
            if k:
                one(k).start()
    relay(4)
    masked = jnp.where(inv[...] >= 0, coeffs[...], 0.0)
    kept[0] = mv[...] - dot_full(tv[...], masked, ((0,), (0,)))
    summed = bands[:, pl.ds(pl.multiple_of(q * 128, 128), 128)].astype(F32)
    for k in range(1, NQ):
        one(k).wait_recv()
        summed = summed + first[k - 1].astype(F32)
    total[...] = summed.astype(BF16)
    for o in far_first:
        two(o).start()
    second[z] = summed.astype(BF16)
    for far, direction, step, sub in forwards:
        if not far:
            core_copy(far, direction, step, sub, 1 - core).wait_recv()
    grad_inputs(x)
    for o in range(1, NZ):
        two_arrived(o).wait_recv()
    summed = second[0].astype(F32)
    for at in range(1, NZ):
        summed = summed + second[at].astype(F32)
    third[q] = (summed / (NZ * NQ)).astype(BF16)
    for k in (3, 2, 1):
        three(k).start()
    relay(5)
    for far, direction, step, sub in forwards:
        if far:
            core_copy(far, direction, step, sub, 1 - core).wait_recv()
    grad_inputs(1 - x)
    for k in range(1, NQ):
        three_arrived(k).wait_recv()
    for at in range(NQ):
        mean[:, at * 128 : at * 128 + 128] = third[at].astype(F32)

    cot_copy().wait_send()
    for o in range(NY):
        act_copy(o).wait_send()
    for direction in range(2):
        for sub in range(SUBS):
            half_copy(direction, sub).wait_send()
            for step in range(3):
                block_copy(direction, step, sub).wait_send()
        for step in range(4):
            if step < 4 - direction:
                piece_copy(direction, step).wait_send()
            for sub in range(2):
                if step < 3 or sub == direction:
                    z_copy(direction, step, sub).wait_send()
    for far, direction, step, sub in forwards:
        core_copy(far, direction, step, sub, core).wait_send()
        if far:
            far_copy(direction, step, sub, x).wait_send()
    for k in range(1, NQ):
        one(k).wait_send()
        three(k).wait_send()
    for o in range(1, NZ):
        two(o).wait_send()


def step(activations, cotangent, weight, momentum, positions, table):
    hbm, vmem = pl.BlockSpec(memory_space=pltpu.HBM), pl.BlockSpec(memory_space=pltpu.VMEM)
    dma = pltpu.SemaphoreType.DMA
    return pl.pallas_call(
        step_kernel,
        out_shape=(
            jax.ShapeDtypeStruct((1, SPAN, KV), F32),
            jax.ShapeDtypeStruct((TOK, FEAT), BF16),
            jax.ShapeDtypeStruct((TOPK, KV), F32),
            jax.ShapeDtypeStruct((SPAN, KV), jnp.int32),
        ),
        in_specs=[hbm] * 6,
        out_specs=(vmem,) * 4,
        scratch_shapes=[
            pltpu.VMEM((TOK, HALF), BF16),
            pltpu.VMEM((TOK, KV), BF16),
            pltpu.VMEM((TOPK, KV), jnp.int32),
            pltpu.VMEM((SPAN, SPAN), F32),
            pltpu.VMEM((SPAN, KV), F32),
            pltpu.VMEM((NY, TOK, SPAN), BF16),
            pltpu.VMEM((TOK, KV), BF16),
            pltpu.VMEM((NY, SPAN, KV), F32),
            pltpu.VMEM((16, 16, 16, KV), BF16),
            pltpu.VMEM((2, SPAN, SPAN), BF16),
            pltpu.VMEM((2, SPAN, SPAN), BF16),
            pltpu.VMEM((2, 3, SPAN, KV), BF16),
            pltpu.VMEM((2, 3, SPAN, KV), BF16),
            pltpu.VMEM((SPAN, KV), F32),
            pltpu.VMEM((TOPK, KV), BF16),
            pltpu.VMEM((3, TOPK, 128), BF16),
            pltpu.VMEM((TOPK, 128), BF16),
            pltpu.VMEM((NZ, TOPK, 128), BF16),
            pltpu.VMEM((NQ, TOPK, 128), BF16),
            dma((6,)),
            dma((9,)), dma((9,)),
            dma((2, SUBS)), dma((2, SUBS)),
            dma((2, 3, SUBS)), dma((2, 3, SUBS)),
            dma((2, 4)), dma((2, 4)),
            dma((2, 4, 2)), dma((2, 4, 2)),
            dma((2, 5, 2)), dma((2, 5, 2)),
            dma((2, 2, 5, 2)), dma((2, 2, 5, 2)),
            dma((3, 8)), dma((3, 8)),
        ],
        compiler_params=pltpu.CompilerParams(
            collective_id=0, has_side_effects=True, vmem_limit_bytes=40 << 20
        ),
        name="step",
    )(activations, cotangent, weight, momentum, positions, table)


def finish_kernel(table, mean, inv, given, moment, update, result, kept, dense, decoded, sem):
    copies = [pltpu.make_async_copy(given, result, sem.at[0]), pltpu.make_async_copy(moment, kept, sem.at[1])]
    for copy in copies:
        copy.start()
    for half in range(2):
        side = pl.ds(half * SPAN, SPAN)
        for column in range(2):
            lanes = pl.ds(half * SPAN + column * 128, 128)
            for r in range(SPAN // 8):
                dense[half, pl.ds(r * 8, 8), pl.ds(column * 128, 128)] = pick_rows(
                    mean[:, lanes], inv[pl.ds(r * 8, 8), lanes], TOPK // 8
                )
        decoded[half] = dot_full(table[...], dense[half], ((0,), (0,))).astype(BF16)
        copies.append(pltpu.make_async_copy(decoded.at[half], update.at[:, side], sem.at[2 + half]))
        copies[-1].start()
    for copy in copies:
        copy.wait()


def finish(table, mean, inv, given, moment):
    hbm, vmem = pl.BlockSpec(memory_space=pltpu.HBM), pl.BlockSpec(memory_space=pltpu.VMEM)
    return pl.pallas_call(
        finish_kernel,
        out_shape=(
            jax.ShapeDtypeStruct((SPAN, KV), BF16),
            jax.ShapeDtypeStruct((TOK, FEAT), BF16),
            jax.ShapeDtypeStruct((1, SPAN, KV), F32),
        ),
        in_specs=[vmem] * 5,
        out_specs=(hbm, hbm, hbm),
        scratch_shapes=[
            pltpu.VMEM((2, SPAN, SPAN), F32),
            pltpu.VMEM((2, SPAN, SPAN), BF16),
            pltpu.SemaphoreType.DMA((4,)),
        ],
        compiler_params=pltpu.CompilerParams(vmem_limit_bytes=8 << 20),
        name="finish",
    )(table, mean, inv, given, moment)


def on_device(activations, cotangent, weight, momentum, positions):
    table = jnp.asarray(transform_table(SPAN))
    held = [
        pltpu.with_memory_space_constraint(array, pltpu.HBM)
        for array in (activations, cotangent, weight.reshape(16, 16, KV), momentum[0], positions[0], table)
    ]
    moment, product, mean, inv = step(*held)
    update, grad_input, kept = finish(table, mean, inv, product, moment)
    return grad_input, kept, update


def solution(mesh):
    placed = (
        P(("dp", "fsdp"), None),
        P(("dp", "fsdp"), None),
        P("fsdp", None),
        P("dp", "fsdp", None),
        P("fsdp", None, None),
    )
    return jax.shard_map(
        on_device,
        mesh=mesh,
        in_specs=placed,
        out_specs=(P(("dp", "fsdp"), None), P("dp", "fsdp", None), P("fsdp", None)),
        check_vma=False,
    )
```

```python
import functools

import jax
import jax.numpy as jnp
import numpy as np
from jax import lax
from jax.experimental import pallas as pl
from jax.experimental.pallas import tpu as pltpu
from jax.sharding import PartitionSpec as P

NZ, NQ, NX, NY = 8, 4, 2, 8
SPAN, KV, TOPK, TOK, FEAT = 256, 512, 32, 192, 4096
HALF = FEAT // NX
SUBS = 4
TOKENS_IN = (((0,), (0,)), ((), ()))
MOMENTUM_DECAY = 0.999
MESH = pl.DeviceIdType.MESH
F32, BF16 = jnp.float32, jnp.bfloat16


def transform_table(length):
    freq = np.arange(length, dtype=np.float64)[:, None]
    place = np.arange(length, dtype=np.float64)[None, :]
    scales = np.where(freq == 0, np.sqrt(1.0 / length), np.sqrt(2.0 / length))
    return (scales * np.cos(np.pi * (2 * place + 1) * freq / (2 * length))).astype(np.float32)


def remote(src, dst, send, recv, dp, fsdp):
    return pltpu.make_async_remote_copy(
        src_ref=src, dst_ref=dst, send_sem=send, recv_sem=recv,
        device_id=(dp, fsdp), device_id_type=MESH,
    )


def meet(peers):
    barrier = pltpu.get_barrier_semaphore()
    for peer in peers:
        pl.semaphore_signal(barrier, inc=1, device_id=peer, device_id_type=MESH)
    pl.semaphore_wait(barrier, len(peers))


def pick_rows(values, where, groups):
    low, high = where & 7, where >> 3
    found = jnp.zeros(where.shape, values.dtype)
    for group in range(groups):
        rows = jnp.take_along_axis(values[group * 8 : group * 8 + 8, :], low, axis=0)
        found = jnp.where(high == group, rows, found)
    return found


def dot_full(left, right, dims):
    return lax.dot_general(
        left, right, (dims, ((), ())), precision=lax.Precision.HIGHEST, preferred_element_type=F32
    )


def step_kernel(
    a, c, w, momentum, positions, table,
    kept, out, mean, inv,
    av, cv, pos, tv, mv, ax, cx, part, full, half_s, half_r, block_s, block_r,
    coeffs, bands, first, total, second, third,
    ls, xs, xr, hs, hr, ys, yr, ws, wr, zs, zr, fs, fr, cs, cr, ss, sr,
):
    d, f = lax.axis_index("dp"), lax.axis_index("fsdp")
    x, y = f // NY, lax.rem(f, NY)
    z, q = d // NQ, lax.rem(d, NQ)
    hi, core = q // 2, lax.rem(q, 2)
    piece = z * 2 + core
    other_x = lax.rem(f + NY, NX * NY)
    other_core = d + 1 - 2 * core
    other_hi = z * NQ + (1 - hi) * 2 + core

    def wrap_y(at):
        return lax.rem(at + 2 * NY, NY)

    def wrap_z(at):
        return lax.rem(at + 2 * NZ, NZ)

    def at_y(step):
        return x * NY + wrap_y(y + step)

    def at_z(step):
        return wrap_z(z + step) * NQ + q

    def at_q(k):
        new_hi = 1 - hi if k // 2 else hi
        new_core = 1 - core if k % 2 else core
        return new_hi * 2 + new_core

    local = [
        pltpu.make_async_copy(positions, pos, ls.at[0]),
        pltpu.make_async_copy(c, cv, ls.at[1]),
        pltpu.make_async_copy(a.at[:, pl.ds(pl.multiple_of(x * HALF, HALF), HALF)], av, ls.at[2]),
        pltpu.make_async_copy(w.at[piece], full.at[f, piece], ls.at[3]),
        pltpu.make_async_copy(table, tv, ls.at[4]),
        pltpu.make_async_copy(momentum, mv, ls.at[5]),
    ]
    for copy in local:
        copy.start()

    meet(
        [(d, other_x), (other_hi, other_x), (d, at_y(1)), (d, at_y(-1)), (at_z(1), f), (at_z(-1), f)]
        + [(z * NQ + at_q(k), f) for k in range(1, NQ)]
    )

    def cot_copy():
        return remote(c, cx, xs.at[8], xr.at[8], d, other_x)

    def act_copy(block):
        columns = pl.ds(pl.multiple_of((1 - x) * HALF + block * SPAN, SPAN), SPAN)
        return remote(a.at[:, columns], ax.at[block], xs.at[block], xr.at[block], d, other_x)

    def piece_copy(direction, step, arriving=0):
        way = 1 - 2 * direction
        ref = full.at[at_y(-(step + arriving) * way), piece]
        first_hop = step == 0 and not arriving
        return remote(
            w.at[piece] if first_hop else ref, ref, ws.at[direction, step], wr.at[direction, step], d, at_y(way)
        )

    def pass_pieces(step):
        for direction in range(2):
            if step - 1 < 4 - direction:
                piece_copy(direction, step - 1, arriving=1).wait_recv()
            if step < 4 - direction:
                piece_copy(direction, step).start()

    far_first = (4, 3, 5, 2, 6, 1, 7)
    for direction in range(2):
        piece_copy(direction, 0).start()
    cot_copy().start()
    for o in (4, 3, -3, 2, -2, 1, -1, 0):
        act_copy(wrap_y(y + o)).start()

    local[0].wait()

    @pl.loop(0, SPAN // 32)
    def _(r):
        rows = pl.ds(pl.multiple_of(r * 32, 32), 32)
        level = lax.broadcasted_iota(jnp.int32, (32, KV), 0) + r * 32
        found = jnp.full((32, KV), -1, jnp.int32)
        for i in range(TOPK):
            row = jnp.broadcast_to(pos[i : i + 1, :], (32, KV))
            found = jnp.where(row == level, i, found)
        inv[rows, :] = found

    pass_pieces(1)

    local[1].wait()
    local[2].wait()

    @pl.loop(0, NY)
    def _(block):
        columns = pl.ds(pl.multiple_of(block * SPAN, SPAN), SPAN)
        part[block] = lax.dot_general(av[:, columns], cv[...], TOKENS_IN, preferred_element_type=F32)

    pass_pieces(2)

    def product(block):
        act_copy(block).wait_recv()
        part[block] += lax.dot_general(ax[block], cx[...], TOKENS_IN, preferred_element_type=F32)

    rows_of = SPAN // SUBS

    def half_copy(direction, sub):
        rows = pl.ds(sub * rows_of, rows_of)
        return remote(
            half_s.at[direction, rows], half_r.at[direction, rows], hs.at[direction, sub], hr.at[direction, sub],
            d, at_y(1 - 2 * direction),
        )

    def block_copy(direction, step, sub):
        rows = pl.ds(sub * rows_of, rows_of)
        return remote(
            block_s.at[direction, step, rows], block_r.at[direction, step, rows],
            ys.at[direction, step, sub], yr.at[direction, step, sub],
            d, at_y(1 - 2 * direction),
        )

    def send_halves():
        block = wrap_y(y + 4)
        for sub in range(SUBS):
            for direction in range(2):
                rows, columns = pl.ds(sub * rows_of, rows_of), pl.ds(direction * SPAN, SPAN)
                half_s[direction, rows] = part[block, rows, columns].astype(BF16)
                half_copy(direction, sub).start()

    def send_blocks(step):
        for sub in range(SUBS):
            for direction in range(2):
                rows = pl.ds(sub * rows_of, rows_of)
                block = wrap_y(y + (3 - step) * (1 - 2 * direction))
                if step == 0:
                    mine, others = pl.ds(direction * SPAN, SPAN), pl.ds((1 - direction) * SPAN, SPAN)
                    half_copy(direction, sub).wait_recv()
                    value = part[block, rows, mine] + half_r[direction, rows].astype(F32)
                    block_s[direction, step, rows, mine] = value.astype(BF16)
                    block_s[direction, step, rows, others] = part[block, rows, others].astype(BF16)
                else:
                    block_copy(direction, step - 1, sub).wait_recv()
                    value = part[block, rows, :] + block_r[direction, step - 1, rows].astype(F32)
                    block_s[direction, step, rows] = value.astype(BF16)
                block_copy(direction, step, sub).start()

    def z_block(direction, step, which):
        return wrap_z(z - step * (1 - 2 * direction)) * 2 + which

    def shards(side, sub):
        return pl.ds(side * 8 + sub * 4, 4)

    def z_copy(direction, step, sub, arriving=0):
        ref = full.at[shards(x, sub), z_block(direction, step + arriving, core)]
        return remote(
            ref, ref, zs.at[direction, step, sub], zr.at[direction, step, sub], at_z(1 - 2 * direction), f
        )

    def far_copy(direction, step, sub, side):
        ref = full.at[shards(side, sub), z_block(direction, step, core)]
        return remote(
            ref, ref, fs.at[direction, step, sub], fr.at[direction, step, sub], other_hi, other_x
        )

    def core_copy(far, direction, step, sub, which):
        side = 1 - x if far else x
        ref = full.at[shards(side, sub), z_block(direction, step, which)]
        return remote(
            ref, ref, cs.at[far, direction, step, sub], cr.at[far, direction, step, sub], other_core, f
        )

    def units(step):
        if step == 0:
            return ((0, 0), (0, 1))
        if step == 4:
            return ((0, 0), (1, 1))
        return ((0, 0), (1, 0), (0, 1), (1, 1))

    def relay(step):
        if step == 0:
            for sub in range(2):
                for direction in range(2):
                    z_copy(direction, 0, sub).start()
        elif step < 5:
            for direction, sub in units(step):
                z_copy(direction, step - 1, sub, arriving=1).wait_recv()
                if step < 3 or (step == 3 and sub == direction):
                    z_copy(direction, step, sub).start()
        if step < 5:
            for direction, sub in units(step):
                far_copy(direction, step, sub, x).start()
                core_copy(0, direction, step, sub, core).start()
        if step > 0:
            for direction, sub in units(step - 1):
                far_copy(direction, step - 1, sub, 1 - x).wait_recv()
                core_copy(1, direction, step - 1, sub, core).start()

    pass_pieces(3)
    cot_copy().wait_recv()
    product(wrap_y(y + 4))
    send_halves()
    local[3].wait()
    pass_pieces(4)
    relay(0)
    for o in (3, -3):
        product(wrap_y(y + o))
    send_blocks(0)
    relay(1)
    for o in (2, -2):
        product(wrap_y(y + o))
    send_blocks(1)
    relay(2)
    for o in (1, -1):
        product(wrap_y(y + o))
    send_blocks(2)
    relay(3)
    product(y)
    local[5].wait()
    mv[...] = MOMENTUM_DECAY * mv[...] + part[y]
    for sub in range(SUBS):
        rows = pl.ds(sub * rows_of, rows_of)
        moment = mv[rows, :]
        for direction in range(2):
            block_copy(direction, 2, sub).wait_recv()
            moment = moment + block_r[direction, 2, rows].astype(F32)
        mv[rows, :] = moment

    def one(k):
        columns = pl.ds(pl.multiple_of(at_q(k) * 128, 128), 128)
        return remote(bands.at[:, columns], first.at[k - 1], ss.at[0, k], sr.at[0, k], z * NQ + at_q(k), f)

    def two(o):
        return remote(total, second.at[z], ss.at[1, o], sr.at[1, o], at_z(o), f)

    def two_arrived(o):
        return remote(total, second.at[wrap_z(z - o)], ss.at[1, o], sr.at[1, o], at_z(o), f)

    def three(k):
        return remote(third.at[q], third.at[q], ss.at[2, k], sr.at[2, k], z * NQ + at_q(k), f)

    def three_arrived(k):
        slot = third.at[at_q(k)]
        return remote(slot, slot, ss.at[2, k], sr.at[2, k], z * NQ + at_q(k), f)

    def grad_inputs(side):
        @pl.loop(0, 4)
        def _(at):
            tile = side * 4 + at
            columns = pl.ds(pl.multiple_of(tile * 512, 512), 512)
            rows = full[pl.ds(tile * 2, 2)].reshape(512, KV)
            out[:, columns] = lax.dot_general(
                cv[...], rows, (((1,), (1,)), ((), ())), preferred_element_type=F32
            ).astype(BF16)

    forwards = [(far, way, step, sub) for step in range(5) for far in range(2) for way, sub in units(step)]
    local[4].wait()
    for to in ((3, 2), (1, 0)):
        side = pl.ds(pl.multiple_of(at_q(to[1]) // 2 * SPAN, SPAN), SPAN)
        coeffs[:, side] = dot_full(tv[...], mv[:, side], ((1,), (0,)))
        for k in to:
            lanes = pl.ds(pl.multiple_of(at_q(k) * 128, 128), 128)
            picked = [
                pick_rows(coeffs[:, lanes], pos[pl.ds(r * 8, 8), lanes], SPAN // 8) for r in range(TOPK // 8)
            ]
            bands[:, lanes] = jnp.concatenate(picked, axis=0).astype(BF16)
            if k:
                one(k).start()
    relay(4)
    summed = bands[:, pl.ds(pl.multiple_of(q * 128, 128), 128)].astype(F32)
    for k in range(1, NQ):
        one(k).wait_recv()
        summed = summed + first[k - 1].astype(F32)
    total[...] = summed.astype(BF16)
    for o in far_first:
        two(o).start()
    second[z] = summed.astype(BF16)
    masked = jnp.where(inv[...] >= 0, coeffs[...], 0.0)
    kept[0] = mv[...] - dot_full(tv[...], masked, ((0,), (0,)))
    for far, direction, step, sub in forwards:
        if not far:
            core_copy(far, direction, step, sub, 1 - core).wait_recv()
    grad_inputs(x)
    for o in range(1, NZ):
        two_arrived(o).wait_recv()
    summed = second[0].astype(F32)
    for at in range(1, NZ):
        summed = summed + second[at].astype(F32)
    third[q] = (summed / (NZ * NQ)).astype(BF16)
    for k in (3, 2, 1):
        three(k).start()
    relay(5)
    for far, direction, step, sub in forwards:
        if far:
            core_copy(far, direction, step, sub, 1 - core).wait_recv()
    grad_inputs(1 - x)
    for k in range(1, NQ):
        three_arrived(k).wait_recv()
    for at in range(NQ):
        mean[:, at * 128 : at * 128 + 128] = third[at].astype(F32)

    cot_copy().wait_send()
    for o in range(NY):
        act_copy(o).wait_send()
    for direction in range(2):
        for sub in range(SUBS):
            half_copy(direction, sub).wait_send()
            for step in range(3):
                block_copy(direction, step, sub).wait_send()
        for step in range(4):
            if step < 4 - direction:
                piece_copy(direction, step).wait_send()
            for sub in range(2):
                if step < 3 or sub == direction:
                    z_copy(direction, step, sub).wait_send()
    for far, direction, step, sub in forwards:
        core_copy(far, direction, step, sub, core).wait_send()
        if far:
            far_copy(direction, step, sub, x).wait_send()
    for k in range(1, NQ):
        one(k).wait_send()
        three(k).wait_send()
    for o in range(1, NZ):
        two(o).wait_send()


def step(activations, cotangent, weight, momentum, positions, table):
    hbm, vmem = pl.BlockSpec(memory_space=pltpu.HBM), pl.BlockSpec(memory_space=pltpu.VMEM)
    dma = pltpu.SemaphoreType.DMA
    return pl.pallas_call(
        step_kernel,
        out_shape=(
            jax.ShapeDtypeStruct((1, SPAN, KV), F32),
            jax.ShapeDtypeStruct((TOK, FEAT), BF16),
            jax.ShapeDtypeStruct((TOPK, KV), F32),
            jax.ShapeDtypeStruct((SPAN, KV), jnp.int32),
        ),
        in_specs=[hbm] * 6,
        out_specs=(vmem,) * 4,
        scratch_shapes=[
            pltpu.VMEM((TOK, HALF), BF16),
            pltpu.VMEM((TOK, KV), BF16),
            pltpu.VMEM((TOPK, KV), jnp.int32),
            pltpu.VMEM((SPAN, SPAN), F32),
            pltpu.VMEM((SPAN, KV), F32),
            pltpu.VMEM((NY, TOK, SPAN), BF16),
            pltpu.VMEM((TOK, KV), BF16),
            pltpu.VMEM((NY, SPAN, KV), F32),
            pltpu.VMEM((16, 16, 16, KV), BF16),
            pltpu.VMEM((2, SPAN, SPAN), BF16),
            pltpu.VMEM((2, SPAN, SPAN), BF16),
            pltpu.VMEM((2, 3, SPAN, KV), BF16),
            pltpu.VMEM((2, 3, SPAN, KV), BF16),
            pltpu.VMEM((SPAN, KV), F32),
            pltpu.VMEM((TOPK, KV), BF16),
            pltpu.VMEM((3, TOPK, 128), BF16),
            pltpu.VMEM((TOPK, 128), BF16),
            pltpu.VMEM((NZ, TOPK, 128), BF16),
            pltpu.VMEM((NQ, TOPK, 128), BF16),
            dma((6,)),
            dma((9,)), dma((9,)),
            dma((2, SUBS)), dma((2, SUBS)),
            dma((2, 3, SUBS)), dma((2, 3, SUBS)),
            dma((2, 4)), dma((2, 4)),
            dma((2, 4, 2)), dma((2, 4, 2)),
            dma((2, 5, 2)), dma((2, 5, 2)),
            dma((2, 2, 5, 2)), dma((2, 2, 5, 2)),
            dma((3, 8)), dma((3, 8)),
        ],
        compiler_params=pltpu.CompilerParams(
            collective_id=0, has_side_effects=True, vmem_limit_bytes=40 << 20
        ),
        name="step",
    )(activations, cotangent, weight, momentum, positions, table)


def finish_kernel(table, mean, inv, given, moment, update, result, kept, dense, decoded, sem):
    copies = [pltpu.make_async_copy(given, result, sem.at[0]), pltpu.make_async_copy(moment, kept, sem.at[1])]
    for copy in copies:
        copy.start()
    for half in range(2):
        side = pl.ds(half * SPAN, SPAN)
        for column in range(2):
            lanes = pl.ds(half * SPAN + column * 128, 128)
            for r in range(SPAN // 8):
                dense[half, pl.ds(r * 8, 8), pl.ds(column * 128, 128)] = pick_rows(
                    mean[:, lanes], inv[pl.ds(r * 8, 8), lanes], TOPK // 8
                )
        decoded[half] = dot_full(table[...], dense[half], ((0,), (0,))).astype(BF16)
        copies.append(pltpu.make_async_copy(decoded.at[half], update.at[:, side], sem.at[2 + half]))
        copies[-1].start()
    for copy in copies:
        copy.wait()


def finish(table, mean, inv, given, moment):
    hbm, vmem = pl.BlockSpec(memory_space=pltpu.HBM), pl.BlockSpec(memory_space=pltpu.VMEM)
    return pl.pallas_call(
        finish_kernel,
        out_shape=(
            jax.ShapeDtypeStruct((SPAN, KV), BF16),
            jax.ShapeDtypeStruct((TOK, FEAT), BF16),
            jax.ShapeDtypeStruct((1, SPAN, KV), F32),
        ),
        in_specs=[vmem] * 5,
        out_specs=(hbm, hbm, hbm),
        scratch_shapes=[
            pltpu.VMEM((2, SPAN, SPAN), F32),
            pltpu.VMEM((2, SPAN, SPAN), BF16),
            pltpu.SemaphoreType.DMA((4,)),
        ],
        compiler_params=pltpu.CompilerParams(vmem_limit_bytes=8 << 20),
        name="finish",
    )(table, mean, inv, given, moment)


def on_device(activations, cotangent, weight, momentum, positions):
    table = jnp.asarray(transform_table(SPAN))
    held = [
        pltpu.with_memory_space_constraint(array, pltpu.HBM)
        for array in (activations, cotangent, weight.reshape(16, 16, KV), momentum[0], positions[0], table)
    ]
    moment, product, mean, inv = step(*held)
    update, grad_input, kept = finish(table, mean, inv, product, moment)
    return grad_input, kept, update


def solution(mesh):
    placed = (
        P(("dp", "fsdp"), None),
        P(("dp", "fsdp"), None),
        P("fsdp", None),
        P("dp", "fsdp", None),
        P("fsdp", None, None),
    )
    return jax.shard_map(
        on_device,
        mesh=mesh,
        in_specs=placed,
        out_specs=(P(("dp", "fsdp"), None), P("dp", "fsdp", None), P("fsdp", None)),
        check_vma=False,
    )
```
